32 devices in a mesh: seg: 2 (over y), ch: 16 (over z, x, core).
Axes of the slice: x: 2, y: 2, z: 4, core: 2. Of those that a mesh axis runs over, the one named last changes fastest.
Arguments:
- strain: float32 [2, 1024, 2048], P('seg', 'ch')
- ref_local: int32 [4, 16], replicated, may hold values from 0 to 127, as said below
- owners: int32 [4], replicated, may hold values from 0 to 15, as said below
Outputs:
- toeplitz_blocks: float32 [64, 2048, 64], P('seg', 'ch')
The draws below stay inside these ranges and needn't reach their ends.
Inputs may be any that keep to these rules, and one draw needn't show every extreme that they name: `ref_local`: each row holds 16 distinct offsets; the first row holds 127. `owners`: the 4 entries are distinct, and one of them is 15.
All inputs are finite; a program needn't handle non-finite values.
Results may differ from the reference program's by a relative error of at most 0.0029.
Values may be sent and summed in bfloat16 or wider, within the bound.
A program may use at most 64 MiB of HBM per device.

```python
import math
import jax
import jax.numpy as jnp
from jax import lax

C = 2048
L = 64
PANELS = 4
PANEL_W = 16
SEGS = 2
S = 1024
C_DEV = 128
R = 64


def draw_strain(key, part):
    keys = jax.random.split(key, 6)
    n_modes = 6
    times = jnp.arange(S, dtype=jnp.float32)[None, :, None]
    freqs = jnp.exp(jax.random.uniform(keys[0], (n_modes,), jnp.float32, math.log(0.003), math.log(0.6)))
    amps = jax.random.normal(keys[1], (SEGS, 1, C, n_modes), jnp.float32) * 0.12
    phases = jax.random.uniform(keys[2], (SEGS, 1, C, n_modes), jnp.float32, -math.pi, math.pi)
    offsets = jax.random.normal(keys[3], (SEGS, 1, C), jnp.float32) * 3.0
    slopes = jax.random.normal(keys[4], (SEGS, 1, C), jnp.float32) * 3.0
    ramp = 2.0 * times / S - 1.0
    signal_sum = offsets + slopes * ramp
    for mode_id in range(n_modes):
        signal_sum = signal_sum + amps[..., mode_id] * jnp.sin(freqs[mode_id] * times + phases[..., mode_id])
    noise = jax.random.normal(keys[5], (SEGS, S, C), jnp.float32)
    return signal_sum + noise


def draw_ref_local(key, part):
    base_key = jax.random.fold_in(key, 11)
    keys = jax.random.split(base_key, PANELS)
    order_keys = jax.random.split(jax.random.fold_in(base_key, 5), PANELS)
    rows = jax.vmap(lambda one_key: jax.random.permutation(one_key, C_DEV)[:PANEL_W])(keys).astype(jnp.int32)
    first_shift = C_DEV - 1 - rows[0, 0]
    shifts = jnp.zeros((PANELS,), jnp.int32).at[0].set(first_shift)
    rows = (rows + shifts[:, None]) % C_DEV
    return jax.vmap(lambda one_key, one_row: jax.random.permutation(one_key, one_row))(order_keys, rows).astype(jnp.int32)


def draw_owners(key, part):
    base_key = jax.random.fold_in(key, 23)
    picked = jax.random.permutation(base_key, C // C_DEV)[:PANELS].astype(jnp.int32)
    n_groups = C // C_DEV
    picked = (picked + (n_groups - 1) - picked[0]) % n_groups
    return jax.random.permutation(jax.random.fold_in(base_key, 7), picked).astype(jnp.int32)


def setup_inputs(seed: int = 0) -> dict:
    streams_of = jax.random.split(jax.random.key(seed), 4)
    strain = draw_strain(jax.random.fold_in(streams_of[3], 71), 0)
    ref_local = draw_ref_local(jax.random.fold_in(streams_of[3], 71), 0)
    owners = draw_owners(jax.random.fold_in(streams_of[3], 71), 0)
    return dict(strain=strain, ref_local=ref_local, owners=owners)


def detrend_cols(series):
    n_total = series.shape[0]
    mid_time = (n_total - 1) / 2.0
    spread = n_total * (n_total * n_total - 1) / 12.0
    centred = (jnp.arange(n_total, dtype=jnp.float32) - mid_time)[:, None]
    level_val = jnp.sum(series, axis=0) / n_total
    slope_val = jnp.sum(centred * series, axis=0) / spread
    return (series - level_val - slope_val * centred).astype(jnp.bfloat16)


def reference(strain, ref_local, owners):
    ref_cols = (owners[:, None] * C_DEV + ref_local).reshape(-1).astype(jnp.int32)

    def one_segment(running, series):
        cleaned = detrend_cols(series).astype(jnp.float32)
        ref_data = jnp.take(cleaned, ref_cols, axis=1)
        padded = jnp.concatenate([cleaned, jnp.zeros((L, C), jnp.float32)], axis=0)

        def one_lag(lag_pos):
            shifted = lax.dynamic_slice_in_dim(padded, lag_pos, S, 0)
            return lax.dot_general(shifted, ref_data, (((0,), (0,)), ((), ())), precision=lax.Precision.HIGHEST)

        lag_covs = lax.map(one_lag, jnp.arange(L, dtype=jnp.int32))
        return running + lag_covs, None

    summed, _ = lax.scan(one_segment, jnp.zeros((L, C, R), jnp.float32), strain)
    lag_ids = jnp.arange(L, dtype=jnp.float32)
    return summed / (SEGS * (S - lag_ids))[:, None, None]
```

```python
import functools
import math

import jax
import jax.numpy as jnp
from jax import lax
from jax.experimental import pallas as pl
from jax.experimental.pallas import tpu as pltpu
from jax.sharding import PartitionSpec as P

L = 64
LANES = 128
SHIFTS = 16
GRANT = 24 * 1024 * 1024
GRANT_LAG = 24 * 1024 * 1024
STEPS = 32000.0
TINY = 1e-33
MESH = pl.DeviceIdType.MESH


def spread_2(block, axis, holder):
    block = jnp.where(lax.axis_index(axis) == holder, block, jnp.zeros_like(block))
    return lax.psum(block, axis)


def detrend_cols(series):
    n_total = series.shape[0]
    mid_time = (n_total - 1) / 2.0
    spread = n_total * (n_total * n_total - 1) / 12.0
    centred = (jnp.arange(n_total, dtype=jnp.float32) - mid_time)[:, None]
    level_val = jnp.sum(series, axis=0) / n_total
    slope_val = jnp.sum(centred * series, axis=0) / spread
    return (series - level_val - slope_val * centred).astype(jnp.bfloat16)


def owner_panels(detrended, ref_local, owners):
    pieces = []
    for panel_id in range(ref_local.shape[0]):
        own_cols = jnp.take(detrended, ref_local[panel_id], axis=1)
        pieces.append(spread_2(own_cols, "ch", owners[panel_id]))
    return jnp.concatenate(pieces, axis=1)


def narrow_blocks(strain, ref_local, owners):
    my_rows = strain[0]
    s_dev, chans = my_rows.shape
    n_ch = lax.axis_size("ch")
    n_seg = lax.axis_size("seg")
    n_total = s_dev * n_ch
    c_dev = chans // n_ch
    series = lax.all_to_all(my_rows, "ch", split_axis=1, concat_axis=0, tiled=True)
    detrended = detrend_cols(series)
    panels = owner_panels(detrended, ref_local, owners)
    width_ref = panels.shape[1]
    padded = jnp.concatenate([detrended, jnp.zeros((L, c_dev), jnp.bfloat16)], axis=0)
    blk_rows = min(512, n_total)
    n_blocks = n_total // blk_rows
    lag_dev = L // n_seg
    lag_count = lax.axis_size("seg") * lag_dev

    def add_block(blk_idx, running):
        blk_start = blk_idx * blk_rows
        window = lax.dynamic_slice_in_dim(padded, blk_start, blk_rows + lag_count - 1, 0)
        lagged = jnp.concatenate(
            [window[lag_off : lag_off + blk_rows] for lag_off in range(lag_count)], axis=1
        )
        ref_block = lax.dynamic_slice_in_dim(panels, blk_start, blk_rows, 0)
        return running + lax.dot_general(
            lagged, ref_block, (((0,), (0,)), ((), ())), preferred_element_type=jnp.float32
        )

    start_acc = jnp.zeros((lag_count * c_dev, width_ref), jnp.float32)
    running = lax.fori_loop(0, n_blocks, add_block, start_acc)
    summed = lax.psum_scatter(
        running.reshape(lag_count, c_dev, width_ref), "seg", scatter_dimension=0, tiled=True
    )
    lag_ids = (lax.axis_index("seg") * lag_dev + jnp.arange(lag_dev, dtype=jnp.int32)).astype(
        jnp.float32
    )
    return summed / (n_seg * (n_total - lag_ids))[:, None, None]


def exchange_kernel(
    n_ch, group, strain_hbm, owners_hbm, local_hbm, d_out, rt_out,
    owners_ref, local_ref, mine, q_out, st_out, q_in, st_in, rline, rb,
    load_sem, small_sem, s_send, s_recv, q_send, q_recv, z_send, z_recv,
    x_send, x_recv, t_send, t_recv, y_send, y_recv,
):
    seg = lax.axis_index("seg")
    me = lax.axis_index("ch")
    other = 1 - seg
    high, low = me // group, me % group
    n_high = n_ch // group
    s_dev = strain_hbm.shape[0]
    c_dev = strain_hbm.shape[1] // n_ch
    n_total = s_dev * n_ch
    n_panels, panel_w = local_ref.shape
    width = n_panels * panel_w
    mid_time = (n_total - 1) / 2.0
    spread = n_total * (n_total * n_total - 1) / 12.0
    mid_dev = (s_dev - 1) / 2.0
    spread_dev = s_dev * (s_dev * s_dev - 1) / 12.0
    cross = list(range(n_ch // 2, n_ch))
    near = list(range(n_ch // 2))

    def partner(k):
        place, bit = me, 1
        while bit <= k:
            if k & bit:
                place = place + (1 - 2 * ((me // bit) % 2)) * bit
            bit *= 2
        return place

    def remote(src, dst, sems, k, seg_to, ch_to):
        copy = pltpu.make_async_remote_copy(
            src_ref=src,
            dst_ref=dst,
            send_sem=sems[0].at[k],
            recv_sem=sems[1].at[k],
            device_id=(seg_to, ch_to),
            device_id_type=MESH,
        )
        copy.start()
        return copy

    loads = []
    for k in cross + near:
        o = partner(k)
        cols = pl.ds(pl.multiple_of(o * c_dev, LANES), c_dev)
        loads.append(pltpu.make_async_copy(strain_hbm.at[:, cols], mine.at[o], load_sem.at[k]))
        loads[-1].start()
    load_owners = pltpu.make_async_copy(owners_hbm, owners_ref, small_sem.at[0])
    load_owners.start()
    load_local = pltpu.make_async_copy(local_hbm, local_ref, small_sem.at[1])
    load_local.start()

    barrier = pltpu.get_barrier_semaphore()
    for k in range(1, n_ch):
        pl.semaphore_signal(barrier, inc=1, device_id=(seg, partner(k)), device_id_type=MESH)
    for k in near:
        pl.semaphore_signal(barrier, inc=1, device_id=(other, partner(k)), device_id_type=MESH)

    d_out[:, n_total:, :] = jnp.zeros((2, L, c_dev), d_out.dtype)
    v_dev = lax.broadcasted_iota(jnp.int32, (s_dev, c_dev), 0).astype(jnp.float32) - mid_dev

    def line_of(block):
        level = jnp.sum(block, axis=0, keepdims=True) / s_dev
        slope = jnp.sum(v_dev[:, : block.shape[1]] * block, axis=0, keepdims=True) / spread_dev
        return level, slope

    for place, k in enumerate(cross + near):
        loads[place].wait()
        o = partner(k)
        block = mine[o]
        level, slope = line_of(block)
        rest = block - level - slope * v_dev
        top = jnp.maximum(jnp.max(jnp.abs(rest), axis=0, keepdims=True), TINY)
        q_out[o] = jnp.round(rest * (STEPS / top)).astype(jnp.int32).astype(jnp.int16)
        st_out[o, 0:3, :] = jnp.concatenate([level, slope, top / STEPS], axis=0)

    load_owners.wait()
    load_local.wait()
    blocks = jnp.concatenate([mine[owners_ref[p]] for p in range(n_panels)], axis=1)
    targets = jnp.concatenate(
        [local_ref[p : p + 1, :] + p * c_dev for p in range(n_panels)], axis=1
    )
    hot = (
        lax.broadcasted_iota(jnp.int32, (n_panels * c_dev, width), 0) == targets
    ).astype(jnp.float32)
    picked = jnp.dot(
        blocks, hot, precision=lax.Precision.HIGHEST, preferred_element_type=jnp.float32
    )
    ref_line = jnp.concatenate(line_of(picked), axis=1)
    st_out[:, 3:4, :] = jnp.broadcast_to(ref_line[None], (n_ch, 1, LANES))
    turned = picked.T
    rline[high] = jnp.concatenate([turned[: width // 2], turned[width // 2 :]], axis=1)
    st_in[seg, me] = st_out[me]

    pl.semaphore_wait(barrier, n_ch - 1 + len(near))

    s_copies = [
        remote(st_out.at[partner(k)], st_in.at[seg, me], (s_send, s_recv), k, seg, partner(k))
        for k in cross + near[1:]
    ]
    z_copies = []
    for k in range(group, n_ch, group):
        z_copies.append(
            remote(rline.at[high], rline.at[high], (z_send, z_recv), k // group, seg, partner(k))
        )
    here, there = {}, {}

    def send_q(k, plane):
        to = (here, there)[plane]
        to[k] = remote(
            q_out.at[partner(k)],
            q_in.at[seg, me],
            (q_send.at[plane], q_recv.at[plane]),
            k,
            other if plane else seg,
            partner(k),
        )

    for k, kk in zip(cross, near):
        send_q(k, 0)
        send_q(kk, 1)
    for k in near[1:]:
        send_q(k, 0)

    def lines(which):
        st = st_in[which]
        centre = (
            lax.broadcasted_iota(jnp.int32, (n_ch, 1, LANES), 0) * s_dev
        ).astype(jnp.float32) + (mid_dev - mid_time)
        level = jnp.sum(st[:, 0:1, :], axis=0) / n_ch
        moment = s_dev * centre * st[:, 0:1, :] + spread_dev * st[:, 1:2, :]
        slope = jnp.sum(moment, axis=0) / spread
        return st, centre, level, slope

    def convert(which, level, slope, k):
        source = partner(k)
        coef = st_in[which, source]
        centre = (source * s_dev).astype(jnp.float32) + (mid_dev - mid_time)
        first = coef[0:1] - level - slope * centre
        second = coef[1:2] - slope
        codes = q_out[me] if which is seg and k == 0 else q_in[which, source]
        rest = codes.astype(jnp.int32).astype(jnp.float32) * coef[2:3]
        rows = pl.ds(pl.multiple_of(source * s_dev, s_dev), s_dev)
        d_out[which, rows, :] = (rest + first + second * v_dev).astype(d_out.dtype)

    for copy in s_copies:
        copy.wait_recv()
    y_copy = remote(st_in.at[seg], st_in.at[seg], (y_send, y_recv), 0, other, me)
    st, centre, level, slope = lines(seg)

    both = jnp.sum(st[:, 3:4, :], axis=0)
    moved = jnp.sum(centre * st[:, 3:4, :], axis=0)
    lane = lax.broadcasted_iota(jnp.int32, (1, LANES), 1)
    ref_stat = jnp.where(
        lane < width,
        both / n_ch,
        (s_dev * pltpu.roll(moved, width, 1) + spread_dev * both) / spread,
    )
    column = jnp.broadcast_to(ref_stat, (8, LANES)).T[:, 0:1]
    half = width // 2
    is_left = lax.broadcasted_iota(jnp.int32, (half, LANES), 1) < s_dev
    ref_level = jnp.where(is_left, column[:half], column[half:width])
    ref_slope = jnp.where(is_left, column[width : width + half], column[width + half :])
    lane_time = lax.broadcasted_iota(jnp.int32, (half, LANES), 1) % s_dev
    for copy in z_copies:
        copy.wait_recv()
    for h in range(n_high):
        times = ((h * group + low) * s_dev + lane_time).astype(jnp.float32) - mid_time
        rb[seg, low, h] = (rline[h] - ref_level - ref_slope * times).astype(rb.dtype)
    x_copies, t_copies = [], []

    def to_twin(j, x):
        block = rb.at[(seg + j) % 2, partner(x) % group]
        t_copies.append(remote(block, block, (t_send, t_recv), j * group + x, seg, partner(1)))

    hops = [(j, x) for j in range(2) for x in range(0, group, 2)]
    mine_rb = rb.at[seg, low]
    for j, x in hops[1:]:
        x_copies.append(
            remote(mine_rb, mine_rb, (x_send, x_recv), j * group + x, (seg + j) % 2, partner(x))
        )
    to_twin(0, 0)

    convert(seg, level, slope, 0)
    for k, kk in zip(cross, near):
        here[k].wait_recv()
        block = q_in.at[seg, partner(k)]
        there[k] = remote(block, block, (q_send.at[1], q_recv.at[1]), k, other, me)
        convert(seg, level, slope, k)
        if kk:
            here[kk].wait_recv()
            convert(seg, level, slope, kk)
    for (j, x), copy in zip(hops[1:], x_copies):
        copy.wait_recv()
        to_twin(j, x)
    y_copy.wait_recv()
    _, _, level, slope = lines(other)
    for k in near:
        there[k].wait_recv()
        convert(other, level, slope, k)
    for copy in t_copies:
        copy.wait_recv()
    full_left = lax.broadcasted_iota(jnp.int32, (half, LANES), 1) < s_dev
    column_id = lax.broadcasted_iota(jnp.int32, (width, n_total), 1)
    for s in range(2):
        tops, lows = [], []
        for i in range(0, n_ch, 2):
            one = rb[s, i % group, i // group].astype(jnp.float32)
            two = rb[s, (i + 1) % group, (i + 1) // group].astype(jnp.float32)
            tops.append(jnp.where(full_left, one, pltpu.roll(two, s_dev, 1)))
            lows.append(jnp.where(full_left, pltpu.roll(one, s_dev, 1), two))
        series = jnp.concatenate(
            [jnp.concatenate(tops, axis=1), jnp.concatenate(lows, axis=1)], axis=0
        )
        for b in range(SHIFTS):
            moved = series
            if b:
                moved = jnp.where(column_id < b, 0.0, pltpu.roll(series, b, 1))
            rt_out[b * width : (b + 1) * width, s * n_total : (s + 1) * n_total] = moved.astype(
                rt_out.dtype
            )
    for k in cross:
        there[k].wait_recv()
        convert(other, level, slope, k)
    for copies in (s_copies, z_copies, here.values(), there.values(), x_copies, t_copies, [y_copy]):
        for copy in copies:
            copy.wait_send()


def lag_kernel(n_seg, d_ref, rt_ref, out_hbm, wide, done, out_sem):
    lag_dev, width, c_dev = out_hbm.shape
    n_total = d_ref.shape[1] - L
    seg = lax.axis_index("seg")
    steps = lag_dev // SHIFTS
    for s in range(n_seg):
        for a in range(steps):
            first = pl.multiple_of(seg * lag_dev + a * SHIFTS, SHIFTS)
            wide[s * n_total : (s + 1) * n_total, a * c_dev : (a + 1) * c_dev] = d_ref[
                s, pl.ds(first, n_total), :
            ]
    base = (seg * lag_dev).astype(jnp.float32)
    quad = 4
    copies = []
    for j in range(SHIFTS // quad):
        rows = quad * width
        total = jnp.dot(
            rt_ref[j * rows : (j + 1) * rows, :], wide[...], preferred_element_type=jnp.float32
        )
        for a in range(steps):
            for b in range(quad):
                k = a * SHIFTS + j * quad + b
                block = total[b * width : (b + 1) * width, a * c_dev : (a + 1) * c_dev]
                done[k] = block * (1.0 / (n_seg * (n_total - (base + k))))
            part = pl.ds(a * SHIFTS + j * quad, quad)
            copies.append(
                pltpu.make_async_copy(
                    done.at[part], out_hbm.at[part], out_sem.at[a * (SHIFTS // quad) + j]
                )
            )
            copies[-1].start()
    for copy in copies:
        copy.wait()


def wide_blocks(strain, ref_local, owners):
    my_rows = strain[0]
    s_dev, chans = my_rows.shape
    n_ch = lax.axis_size("ch")
    n_seg = lax.axis_size("seg")
    n_total = s_dev * n_ch
    c_dev = chans // n_ch
    group = max(g for g in range(1, math.isqrt(n_ch) + 1) if n_ch % g == 0)
    n_high = n_ch // group
    width = ref_local.shape[0] * ref_local.shape[1]
    vmem = pl.BlockSpec(memory_space=pltpu.VMEM)
    hbm = pl.BlockSpec(memory_space=pltpu.HBM)
    dma = pltpu.SemaphoreType.DMA
    d_all, rt_all = pl.pallas_call(
        functools.partial(exchange_kernel, n_ch, group),
        out_shape=(
            jax.ShapeDtypeStruct((n_seg, n_total + L, c_dev), jnp.bfloat16),
            jax.ShapeDtypeStruct((SHIFTS * width, n_seg * n_total), jnp.bfloat16),
        ),
        in_specs=[hbm] * 3,
        out_specs=(vmem, vmem),
        scratch_shapes=[
            pltpu.SMEM(owners.shape, jnp.int32),
            pltpu.VMEM(ref_local.shape, jnp.int32),
            pltpu.VMEM((n_ch, s_dev, c_dev), jnp.float32),
            pltpu.VMEM((n_ch, s_dev, c_dev), jnp.int16),
            pltpu.VMEM((n_ch, 4, c_dev), jnp.float32),
            pltpu.VMEM((n_seg, n_ch, s_dev, c_dev), jnp.int16),
            pltpu.VMEM((n_seg, n_ch, 4, c_dev), jnp.float32),
            pltpu.VMEM((n_high, width // 2, LANES), jnp.float32),
            pltpu.VMEM((n_seg, group, n_high, width // 2, LANES), jnp.bfloat16),
            dma((n_ch,)), dma((2,)),
            dma((n_ch,)), dma((n_ch,)),
            dma((n_seg, n_ch)), dma((n_seg, n_ch)),
            dma((n_high,)), dma((n_high,)),
            dma((n_seg * group,)), dma((n_seg * group,)),
            dma((n_seg * group,)), dma((n_seg * group,)),
            dma((1,)), dma((1,)),
        ],
        compiler_params=pltpu.CompilerParams(
            collective_id=0, has_side_effects=True, vmem_limit_bytes=GRANT
        ),
    )(my_rows, owners, ref_local)
    turned = pl.pallas_call(
        functools.partial(lag_kernel, n_seg),
        out_shape=jax.ShapeDtypeStruct((L // n_seg, width, c_dev), jnp.float32),
        in_specs=[vmem, vmem],
        out_specs=hbm,
        scratch_shapes=[
            pltpu.VMEM((n_seg * n_total, L // n_seg // SHIFTS * c_dev), jnp.bfloat16),
            pltpu.VMEM((L // n_seg, width, c_dev), jnp.float32),
            dma((L // n_seg // 4,)),
        ],
        compiler_params=pltpu.CompilerParams(vmem_limit_bytes=GRANT_LAG),
    )(d_all, rt_all)
    return turned.transpose(0, 2, 1)


def solution(mesh):
    n_seg, n_ch = mesh.shape["seg"], mesh.shape["ch"]

    def per_device(strain, ref_local, owners):
        s_dev, chans = strain.shape[1:]
        fits = (
            chans == n_ch * LANES
            and n_seg == 2
            and (L // n_seg) % SHIFTS == 0
            and 2 * s_dev == LANES
            and n_ch >= 4
            and n_ch & (n_ch - 1) == 0
            and 2 * ref_local.size == LANES
        )
        return (wide_blocks if fits else narrow_blocks)(strain, ref_local, owners)

    in_specs = (P("seg", "ch", None), P(), P())
    out_specs = P("seg", "ch", None)
    return jax.shard_map(
        per_device, mesh=mesh, in_specs=in_specs, out_specs=out_specs, check_vma=False
    )
```

```python
import functools
import math

import jax
import jax.numpy as jnp
from jax import lax
from jax.experimental import pallas as pl
from jax.experimental.pallas import tpu as pltpu
from jax.sharding import PartitionSpec as P

L = 64
LANES = 128
SHIFTS = 16
GRANT = 24 * 1024 * 1024
HOP_AT = 5
STEPS = 32000.0
TINY = 1e-33
MESH = pl.DeviceIdType.MESH


def spread_2(block, axis, holder):
    block = jnp.where(lax.axis_index(axis) == holder, block, jnp.zeros_like(block))
    return lax.psum(block, axis)


def detrend_cols(series):
    n_total = series.shape[0]
    mid_time = (n_total - 1) / 2.0
    spread = n_total * (n_total * n_total - 1) / 12.0
    centred = (jnp.arange(n_total, dtype=jnp.float32) - mid_time)[:, None]
    level_val = jnp.sum(series, axis=0) / n_total
    slope_val = jnp.sum(centred * series, axis=0) / spread
    return (series - level_val - slope_val * centred).astype(jnp.bfloat16)


def owner_panels(detrended, ref_local, owners):
    pieces = []
    for panel_id in range(ref_local.shape[0]):
        own_cols = jnp.take(detrended, ref_local[panel_id], axis=1)
        pieces.append(spread_2(own_cols, "ch", owners[panel_id]))
    return jnp.concatenate(pieces, axis=1)


def narrow_blocks(strain, ref_local, owners):
    my_rows = strain[0]
    s_dev, chans = my_rows.shape
    n_ch = lax.axis_size("ch")
    n_seg = lax.axis_size("seg")
    n_total = s_dev * n_ch
    c_dev = chans // n_ch
    series = lax.all_to_all(my_rows, "ch", split_axis=1, concat_axis=0, tiled=True)
    detrended = detrend_cols(series)
    panels = owner_panels(detrended, ref_local, owners)
    width_ref = panels.shape[1]
    padded = jnp.concatenate([detrended, jnp.zeros((L, c_dev), jnp.bfloat16)], axis=0)
    blk_rows = min(512, n_total)
    n_blocks = n_total // blk_rows
    lag_dev = L // n_seg
    lag_count = lax.axis_size("seg") * lag_dev

    def add_block(blk_idx, running):
        blk_start = blk_idx * blk_rows
        window = lax.dynamic_slice_in_dim(padded, blk_start, blk_rows + lag_count - 1, 0)
        lagged = jnp.concatenate(
            [window[lag_off : lag_off + blk_rows] for lag_off in range(lag_count)], axis=1
        )
        ref_block = lax.dynamic_slice_in_dim(panels, blk_start, blk_rows, 0)
        return running + lax.dot_general(
            lagged, ref_block, (((0,), (0,)), ((), ())), preferred_element_type=jnp.float32
        )

    start_acc = jnp.zeros((lag_count * c_dev, width_ref), jnp.float32)
    running = lax.fori_loop(0, n_blocks, add_block, start_acc)
    summed = lax.psum_scatter(
        running.reshape(lag_count, c_dev, width_ref), "seg", scatter_dimension=0, tiled=True
    )
    lag_ids = (lax.axis_index("seg") * lag_dev + jnp.arange(lag_dev, dtype=jnp.int32)).astype(
        jnp.float32
    )
    return summed / (n_seg * (n_total - lag_ids))[:, None, None]


def fused_kernel(
    n_ch, group, strain_ref, owners_hbm, local_ref, out_ref,
    owners_ref, mine, q_out, st_out, q_in, st_in, rline, rb, wide, rt, acc,
    small_sem, s_send, s_recv, q_send, q_recv, z_send, z_recv,
    x_send, x_recv, t_send, t_recv, y_send, y_recv,
):
    seg = lax.axis_index("seg")
    me = lax.axis_index("ch")
    other = 1 - seg
    high, low = me // group, me % group
    n_high = n_ch // group
    s_dev = strain_ref.shape[0]
    c_dev = strain_ref.shape[1] // n_ch
    n_total = s_dev * n_ch
    n_panels, panel_w = local_ref.shape
    width = n_panels * panel_w
    lag_dev = out_ref.shape[0]
    steps = lag_dev // SHIFTS
    mid_time = (n_total - 1) / 2.0
    spread = n_total * (n_total * n_total - 1) / 12.0
    mid_dev = (s_dev - 1) / 2.0
    spread_dev = s_dev * (s_dev * s_dev - 1) / 12.0
    half = width // 2
    upper = me // (n_ch // 2)

    def flip(place, k):
        bit = 1
        while bit <= k:
            if k & bit:
                place = place + (1 - 2 * ((me // bit) % 2)) * bit
            bit *= 2
        return place

    def partner(k):
        return flip(me, k)

    def far(p):
        row = (1 - upper) * (n_high // 2) + p // group
        return row * group + flip(low, p % group)

    near = [partner(k) for k in range(n_ch // 2)]
    cross = [far(p) for p in range(n_ch // 2)]

    def remote(src, dst, sems, k_send, k_recv, seg_to, ch_to):
        return pltpu.make_async_remote_copy(
            src_ref=src,
            dst_ref=dst,
            send_sem=sems[0].at[k_send],
            recv_sem=sems[1].at[k_recv],
            device_id=(seg_to, ch_to),
            device_id_type=MESH,
        )

    sent = []

    def send(*args):
        copy = remote(*args)
        copy.start()
        sent.append(copy)

    load_owners = pltpu.make_async_copy(owners_hbm, owners_ref, small_sem.at[0])
    load_owners.start()
    barrier = pltpu.get_barrier_semaphore()
    for place in cross + near[1:]:
        pl.semaphore_signal(barrier, inc=1, device_id=(seg, place), device_id_type=MESH)
    for place in near:
        pl.semaphore_signal(barrier, inc=1, device_id=(other, place), device_id_type=MESH)

    for s in range(2):
        wide[s, n_total:, :] = jnp.zeros((L, steps * c_dev), wide.dtype)
    v_dev = lax.broadcasted_iota(jnp.int32, (s_dev, c_dev), 0).astype(jnp.float32) - mid_dev

    def code(block):
        v = v_dev[:, : block.shape[1]]
        level = jnp.sum(block, axis=0, keepdims=True) / s_dev
        slope = jnp.sum(v * block, axis=0, keepdims=True) / spread_dev
        rest = block - level - slope * v
        top = jnp.maximum(jnp.max(jnp.abs(rest), axis=0, keepdims=True), TINY)
        return level, slope, top / STEPS, jnp.round(rest * (STEPS / top))

    for o in range(n_ch):
        block = strain_ref[:, o * c_dev : (o + 1) * c_dev]
        mine[o] = block
        level, slope, scale, codes = code(block)
        q_out[o] = codes.astype(jnp.int32).astype(jnp.int16)
        st_out[o, 0:3, :] = jnp.concatenate([level, slope, scale], axis=0)

    load_owners.wait()
    blocks = jnp.concatenate(
        [mine[owners_ref[p]] for p in range(n_panels)],
        axis=1,
    )
    targets = jnp.concatenate(
        [local_ref[p : p + 1, :] + p * c_dev for p in range(n_panels)], axis=1
    )
    hot = (
        lax.broadcasted_iota(jnp.int32, (n_panels * c_dev, width), 0) == targets
    ).astype(jnp.float32)
    picked = jnp.dot(
        blocks, hot, precision=lax.Precision.HIGHEST, preferred_element_type=jnp.float32
    )
    level, slope, scale, codes = code(picked)
    ref_rows = jnp.concatenate(
        [jnp.concatenate([level, slope], axis=1), jnp.concatenate([scale, scale], axis=1)], axis=0
    )
    st_out[:, 3:5, :] = jnp.broadcast_to(ref_rows[None], (n_ch, 2, LANES))
    turned = codes.T
    rline[high] = (
        jnp.concatenate([turned[:half], turned[half:]], axis=1)
        .astype(jnp.int32)
        .astype(jnp.int16)
    )
    st_in[seg, me] = st_out[me]

    pl.semaphore_wait(barrier, n_ch - 1 + len(near))

    for place in cross + near[1:]:
        send(st_out.at[place], st_in.at[seg, me], (s_send, s_recv), place, me, seg, place)
    for k in range(group, n_ch, group):
        block = rline.at[high]
        send(block, block, (z_send, z_recv), k // group, k // group, seg, partner(k))
    in_q = (q_send.at[0], q_recv.at[0])
    out_q = (q_send.at[1], q_recv.at[1])
    for place, direct in zip(cross, near):
        send(q_out.at[place], q_in.at[seg, me], in_q, place, me, seg, place)
        send(q_out.at[direct], q_in.at[seg, me], out_q, direct, me, other, direct)
    for place in near[1:]:
        send(q_out.at[place], q_in.at[seg, me], in_q, place, me, seg, place)

    def lines(which):
        st = st_in[which]
        centre = (
            lax.broadcasted_iota(jnp.int32, (n_ch, 1, LANES), 0) * s_dev
        ).astype(jnp.float32) + (mid_dev - mid_time)
        level = jnp.sum(st[:, 0:1, :], axis=0) / n_ch
        moment = s_dev * centre * st[:, 0:1, :] + spread_dev * st[:, 1:2, :]
        slope = jnp.sum(moment, axis=0) / spread
        return st, centre, level, slope

    def convert(which, level, slope, source, codes):
        coef = st_in[which, source]
        centre = (source * s_dev).astype(jnp.float32) + (mid_dev - mid_time)
        first = coef[0:1] - level - slope * centre
        second = coef[1:2] - slope
        rest = codes.astype(jnp.int32).astype(jnp.float32) * coef[2:3]
        block = (rest + first + second * v_dev).astype(wide.dtype)
        for a in range(steps):
            row = L + source * s_dev - seg * lag_dev - a * SHIFTS
            rows = pl.ds(pl.multiple_of(row, SHIFTS), s_dev)
            wide[which, rows, a * c_dev : (a + 1) * c_dev] = block

    def arrive(sems, buf, k):
        remote(buf, buf, sems, k, k, seg, partner(1)).wait_recv()

    for place in cross + near[1:]:
        arrive((s_send, s_recv), st_in.at[seg, place], place)
    send(st_in.at[seg], st_in.at[seg], (y_send, y_recv), 0, 0, other, me)
    st, centre, level, slope = lines(seg)

    both = jnp.sum(st[:, 3:4, :], axis=0)
    moved = jnp.sum(centre * st[:, 3:4, :], axis=0)
    lane = lax.broadcasted_iota(jnp.int32, (1, LANES), 1)
    ref_stat = jnp.where(
        lane < width,
        both / n_ch,
        (s_dev * pltpu.roll(moved, width, 1) + spread_dev * both) / spread,
    )
    ref_slope = pltpu.roll(ref_stat, width, 1)
    firsts, scales = [], []
    for h in range(n_high):
        source = h * group + low
        mid = (source * s_dev).astype(jnp.float32) + (mid_dev - mid_time)
        coef = st_in[seg, source]
        firsts.append(coef[3:4] - jnp.where(lane < width, ref_stat + mid * ref_slope, ref_stat))
        scales.append(coef[4:5])
    columns = jnp.concatenate(firsts + scales, axis=0)
    columns = jnp.concatenate([columns] * (8 // (2 * n_high)), axis=0).T
    is_left = lax.broadcasted_iota(jnp.int32, (half, LANES), 1) < s_dev
    lane_time = (
        lax.broadcasted_iota(jnp.int32, (half, LANES), 1) % s_dev
    ).astype(jnp.float32) - mid_dev

    def spread_out(column, top):
        return jnp.where(is_left, column[top : top + half], column[top + half : top + width])

    for k in range(group, n_ch, group):
        arrive((z_send, z_recv), rline.at[partner(k) // group], k // group)
    for h in range(n_high):
        first = spread_out(columns[:, h : h + 1], 0)
        second = spread_out(columns[:, h : h + 1], width)
        scale = spread_out(columns[:, n_high + h : n_high + h + 1], 0)
        codes = rline[h].astype(jnp.int32).astype(jnp.float32)
        rb[seg, low, h] = (codes * scale + first + second * lane_time).astype(rb.dtype)

    def to_twin(j, x):
        block = rb.at[(seg + j) % 2, partner(x) % group]
        send(block, block, (t_send, t_recv), j * group + x, j * group + x, seg, partner(1))

    hops = [(j, x) for j in range(2) for x in range(0, group, 2)]
    mine_rb = rb.at[seg, low]
    for j, x in hops[1:]:
        k = j * group + x
        send(mine_rb, mine_rb, (x_send, x_recv), k, k, (seg + j) % 2, partner(x))
    to_twin(0, 0)

    convert(seg, level, slope, me, q_out[me])
    for p, place in enumerate(cross):
        block = q_in.at[seg, place]
        arrive(in_q, block, place)
        send(block, block, out_q, place, place, other, me)
        convert(seg, level, slope, place, q_in[seg, place])
        if p == HOP_AT:
            for j, x in hops[1:]:
                arrive((x_send, x_recv), rb.at[(seg + j) % 2, partner(x) % group], j * group + x)
                to_twin(j, x)
    for place in near[1:]:
        arrive(in_q, q_in.at[seg, place], place)
        convert(seg, level, slope, place, q_in[seg, place])
    arrive((y_send, y_recv), st_in.at[other], 0)
    _, _, level, slope = lines(other)
    for j, x in hops:
        arrive((t_send, t_recv), rb.at[(seg + j) % 2, partner(x + 1) % group], j * group + x)

    column_id = lax.broadcasted_iota(jnp.int32, (width, n_total), 1)
    for s in range(2):
        tops, lows = [], []
        for i in range(0, n_ch, 2):
            one = rb[s, i % group, i // group].astype(jnp.float32)
            two = rb[s, (i + 1) % group, (i + 1) // group].astype(jnp.float32)
            tops.append(jnp.where(is_left, one, pltpu.roll(two, s_dev, 1)))
            lows.append(jnp.where(is_left, pltpu.roll(one, s_dev, 1), two))
        series = jnp.concatenate(
            [jnp.concatenate(tops, axis=1), jnp.concatenate(lows, axis=1)], axis=0
        )
        for b in range(SHIFTS):
            moved = series
            if b:
                moved = jnp.where(column_id < b, 0.0, pltpu.roll(series, b, 1))
            rt[s, b * width : (b + 1) * width, :] = moved.astype(rt.dtype)

    quad = 4
    rows = quad * width

    def product(which, j):
        return jnp.dot(
            rt[which, j * rows : (j + 1) * rows, :],
            wide[which, L : L + n_total, :],
            preferred_element_type=jnp.float32,
        )

    for j in range(SHIFTS // quad):
        acc[j] = product(seg, j)
    for place in near:
        block = q_in.at[other, place]
        arrive(out_q, block, place)
        convert(other, level, slope, place, q_in[other, place])
    for place in cross:
        block = q_in.at[other, place]
        arrive(out_q, block, place)
        convert(other, level, slope, place, q_in[other, place])
    base = (seg * lag_dev).astype(jnp.float32)
    for j in range(SHIFTS // quad):
        total = acc[j] + product(other, j)
        for a in range(steps):
            for b in range(quad):
                k = a * SHIFTS + j * quad + b
                block = total[b * width : (b + 1) * width, a * c_dev : (a + 1) * c_dev]
                out_ref[k] = block * (1.0 / (2 * (n_total - (base + k))))
    for copy in sent:
        copy.wait_send()


def wide_blocks(strain, ref_local, owners):
    my_rows = strain[0]
    s_dev, chans = my_rows.shape
    n_ch = lax.axis_size("ch")
    n_seg = lax.axis_size("seg")
    n_total = s_dev * n_ch
    c_dev = chans // n_ch
    group = max(g for g in range(1, math.isqrt(n_ch) + 1) if n_ch % g == 0)
    n_high = n_ch // group
    width = ref_local.shape[0] * ref_local.shape[1]
    lag_dev = L // n_seg
    steps = lag_dev // SHIFTS
    vmem = pl.BlockSpec(memory_space=pltpu.VMEM)
    hbm = pl.BlockSpec(memory_space=pltpu.HBM)
    dma = pltpu.SemaphoreType.DMA
    turned = pl.pallas_call(
        functools.partial(fused_kernel, n_ch, group),
        out_shape=jax.ShapeDtypeStruct((lag_dev, width, c_dev), jnp.float32),
        in_specs=[vmem, hbm, vmem],
        out_specs=vmem,
        scratch_shapes=[
            pltpu.SMEM(owners.shape, jnp.int32),
            pltpu.VMEM((n_ch, s_dev, c_dev), jnp.float32),
            pltpu.VMEM((n_ch, s_dev, c_dev), jnp.int16),
            pltpu.VMEM((n_ch, 5, c_dev), jnp.float32),
            pltpu.VMEM((n_seg, n_ch, s_dev, c_dev), jnp.int16),
            pltpu.VMEM((n_seg, n_ch, 5, c_dev), jnp.float32),
            pltpu.VMEM((n_high, width // 2, LANES), jnp.int16),
            pltpu.VMEM((n_seg, group, n_high, width // 2, LANES), jnp.bfloat16),
            pltpu.VMEM((n_seg, L + n_total, steps * c_dev), jnp.bfloat16),
            pltpu.VMEM((n_seg, SHIFTS * width, n_total), jnp.bfloat16),
            pltpu.VMEM((SHIFTS // 4, 4 * width, steps * c_dev), jnp.float32),
            dma((1,)),
            dma((n_ch,)), dma((n_ch,)),
            dma((n_seg, n_ch)), dma((n_seg, n_ch)),
            dma((n_high,)), dma((n_high,)),
            dma((n_seg * group,)), dma((n_seg * group,)),
            dma((n_seg * group,)), dma((n_seg * group,)),
            dma((1,)), dma((1,)),
        ],
        compiler_params=pltpu.CompilerParams(
            collective_id=0, has_side_effects=True, vmem_limit_bytes=GRANT
        ),
    )(my_rows, owners, ref_local)
    return turned.transpose(0, 2, 1)


def solution(mesh):
    n_seg, n_ch = mesh.shape["seg"], mesh.shape["ch"]

    def per_device(strain, ref_local, owners):
        s_dev, chans = strain.shape[1:]
        fits = (
            chans == n_ch * LANES
            and n_seg == 2
            and (L // n_seg) % SHIFTS == 0
            and 2 * s_dev == LANES
            and n_ch >= 4
            and 8 % (2 * (n_ch // max(g for g in range(1, math.isqrt(n_ch) + 1) if n_ch % g == 0))) == 0
            and n_ch & (n_ch - 1) == 0
            and 2 * ref_local.size == LANES
        )
        return (wide_blocks if fits else narrow_blocks)(strain, ref_local, owners)

    in_specs = (P("seg", "ch", None), P(), P())
    out_specs = P("seg", "ch", None)
    return jax.shard_map(
        per_device, mesh=mesh, in_specs=in_specs, out_specs=out_specs, check_vma=False
    )
```

```python
import functools
import math

import jax
import jax.numpy as jnp
from jax import lax
from jax.experimental import pallas as pl
from jax.experimental.pallas import tpu as pltpu
from jax.sharding import PartitionSpec as P

L = 64
LANES = 128
SHIFTS = 16
GRANT = 24 * 1024 * 1024
HOP_AT = 5
STEPS = 32000.0
TINY = 1e-33
MESH = pl.DeviceIdType.MESH


def spread_2(block, axis, holder):
    block = jnp.where(lax.axis_index(axis) == holder, block, jnp.zeros_like(block))
    return lax.psum(block, axis)


def detrend_cols(series):
    n_total = series.shape[0]
    mid_time = (n_total - 1) / 2.0
    spread = n_total * (n_total * n_total - 1) / 12.0
    centred = (jnp.arange(n_total, dtype=jnp.float32) - mid_time)[:, None]
    level_val = jnp.sum(series, axis=0) / n_total
    slope_val = jnp.sum(centred * series, axis=0) / spread
    return (series - level_val - slope_val * centred).astype(jnp.bfloat16)


def owner_panels(detrended, ref_local, owners):
    pieces = []
    for panel_id in range(ref_local.shape[0]):
        own_cols = jnp.take(detrended, ref_local[panel_id], axis=1)
        pieces.append(spread_2(own_cols, "ch", owners[panel_id]))
    return jnp.concatenate(pieces, axis=1)


def narrow_blocks(strain, ref_local, owners):
    my_rows = strain[0]
    s_dev, chans = my_rows.shape
    n_ch = lax.axis_size("ch")
    n_seg = lax.axis_size("seg")
    n_total = s_dev * n_ch
    c_dev = chans // n_ch
    series = lax.all_to_all(my_rows, "ch", split_axis=1, concat_axis=0, tiled=True)
    detrended = detrend_cols(series)
    panels = owner_panels(detrended, ref_local, owners)
    width_ref = panels.shape[1]
    padded = jnp.concatenate([detrended, jnp.zeros((L, c_dev), jnp.bfloat16)], axis=0)
    blk_rows = min(512, n_total)
    n_blocks = n_total // blk_rows
    lag_dev = L // n_seg
    lag_count = lax.axis_size("seg") * lag_dev

    def add_block(blk_idx, running):
        blk_start = blk_idx * blk_rows
        window = lax.dynamic_slice_in_dim(padded, blk_start, blk_rows + lag_count - 1, 0)
        lagged = jnp.concatenate(
            [window[lag_off : lag_off + blk_rows] for lag_off in range(lag_count)], axis=1
        )
        ref_block = lax.dynamic_slice_in_dim(panels, blk_start, blk_rows, 0)
        return running + lax.dot_general(
            lagged, ref_block, (((0,), (0,)), ((), ())), preferred_element_type=jnp.float32
        )

    start_acc = jnp.zeros((lag_count * c_dev, width_ref), jnp.float32)
    running = lax.fori_loop(0, n_blocks, add_block, start_acc)
    summed = lax.psum_scatter(
        running.reshape(lag_count, c_dev, width_ref), "seg", scatter_dimension=0, tiled=True
    )
    lag_ids = (lax.axis_index("seg") * lag_dev + jnp.arange(lag_dev, dtype=jnp.int32)).astype(
        jnp.float32
    )
    return summed / (n_seg * (n_total - lag_ids))[:, None, None]


def fused_kernel(
    n_ch, group, width, strain_ref, picks_ref, out_ref,
    owners_ref, mine, q_out, st_out, q_in, st_in, rq, wide_here, wide_there, rt_here, rt_there, acc,
    small_sem, s_send, s_recv, q_send, q_recv, z_send, z_recv,
    x_send, x_recv, t_send, t_recv, y_send, y_recv,
):
    seg = lax.axis_index("seg")
    me = lax.axis_index("ch")
    other = 1 - seg
    high, low = me // group, me % group
    n_high = n_ch // group
    s_dev = strain_ref.shape[0]
    c_dev = strain_ref.shape[1] // n_ch
    n_total = s_dev * n_ch
    n_panels = picks_ref.shape[0]
    panel_w = width // n_panels
    lag_dev = out_ref.shape[0]
    steps = lag_dev // SHIFTS
    mid_time = (n_total - 1) / 2.0
    spread = n_total * (n_total * n_total - 1) / 12.0
    mid_dev = (s_dev - 1) / 2.0
    spread_dev = s_dev * (s_dev * s_dev - 1) / 12.0
    half = width // 2
    upper = me // (n_ch // 2)

    def flip(place, k):
        bit = 1
        while bit <= k:
            if k & bit:
                place = place + (1 - 2 * ((me // bit) % 2)) * bit
            bit *= 2
        return place

    def partner(k):
        return flip(me, k)

    def far(p):
        row = (1 - upper) * (n_high // 2) + p // group
        return row * group + flip(low, p % group)

    near = [partner(k) for k in range(n_ch // 2)]
    cross = [far(p) for p in range(n_ch // 2)]

    def remote(src, dst, sems, k_send, k_recv, seg_to, ch_to):
        return pltpu.make_async_remote_copy(
            src_ref=src,
            dst_ref=dst,
            send_sem=sems[0].at[k_send],
            recv_sem=sems[1].at[k_recv],
            device_id=(seg_to, ch_to),
            device_id_type=MESH,
        )

    sent = []

    def send(*args):
        copy = remote(*args)
        copy.start()
        sent.append(copy)

    load_owners = pltpu.make_async_copy(picks_ref, owners_ref, small_sem.at[0])
    load_owners.start()
    barrier = pltpu.get_barrier_semaphore()
    for place in cross + near[1:]:
        pl.semaphore_signal(barrier, inc=1, device_id=(seg, place), device_id_type=MESH)
    for place in near:
        pl.semaphore_signal(barrier, inc=1, device_id=(other, place), device_id_type=MESH)

    for wide in (wide_here, wide_there):
        wide[n_total:, :] = jnp.zeros((L, steps * c_dev), wide.dtype)
    v_dev = lax.broadcasted_iota(jnp.int32, (s_dev, c_dev), 0).astype(jnp.float32) - mid_dev

    def code(block):
        v = v_dev[:, : block.shape[1]]
        level = jnp.sum(block, axis=0, keepdims=True) / s_dev
        slope = jnp.sum(v * block, axis=0, keepdims=True) / spread_dev
        rest = block - level - slope * v
        top = jnp.maximum(jnp.max(jnp.abs(rest), axis=0, keepdims=True), TINY)
        return level, slope, top / STEPS, jnp.round(rest * (STEPS / top))

    for o in range(n_ch):
        block = strain_ref[:, o * c_dev : (o + 1) * c_dev]
        mine[o] = block
        level, slope, scale, codes = code(block)
        q_out[o] = codes.astype(jnp.int32).astype(jnp.int16)
        st_out[o, 0:3, :] = jnp.concatenate([level, slope, scale], axis=0)

    load_owners.wait()
    blocks = jnp.concatenate(
        [mine[owners_ref[p, panel_w]] for p in range(n_panels)],
        axis=1,
    )
    targets = jnp.concatenate(
        [picks_ref[p : p + 1, :panel_w] + p * c_dev for p in range(n_panels)], axis=1
    )
    hot = (
        lax.broadcasted_iota(jnp.int32, (n_panels * c_dev, width), 0) == targets
    ).astype(jnp.float32)
    picked = jnp.dot(
        blocks, hot, precision=lax.Precision.HIGHEST, preferred_element_type=jnp.float32
    )
    level, slope, scale, codes = code(picked)
    ref_rows = jnp.concatenate(
        [jnp.concatenate([level, slope], axis=1), jnp.concatenate([scale, scale], axis=1)], axis=0
    )
    st_out[:, 3:5, :] = jnp.broadcast_to(ref_rows[None], (n_ch, 2, LANES))
    turned = codes.T
    rq[seg, low, high] = (
        jnp.concatenate([turned[:half], turned[half:]], axis=1)
        .astype(jnp.int32)
        .astype(jnp.int16)
    )
    st_in[seg, me] = st_out[me]

    pl.semaphore_wait(barrier, n_ch - 1 + len(near))

    hops = [(j, x) for j in range(2) for x in range(0, group, 2)]

    def hop_refs(h, k):
        block = rq.at[seg, low, h]
        for place, (j, x) in enumerate(hops[1:]):
            sem = place * n_high + k
            send(block, block, (x_send, x_recv), sem, sem, (seg + j) % 2, partner(x))

    def to_twin(place):
        j, x = hops[place]
        block = rq.at[(seg + j) % 2, partner(x) % group]
        send(block, block, (t_send, t_recv), place, place, seg, partner(1))

    z_ks = range(group, n_ch, group)
    for k in z_ks:
        block = rq.at[seg, low, high]
        send(block, block, (z_send, z_recv), k // group, k // group, seg, partner(k))
    hop_refs(high, 0)
    for place in cross + near[1:]:
        send(st_out.at[place], st_in.at[seg, me], (s_send, s_recv), place, me, seg, place)
    in_q = (q_send.at[0], q_recv.at[0])
    out_q = (q_send.at[1], q_recv.at[1])
    for place, direct in zip(cross, near):
        send(q_out.at[place], q_in.at[seg, me], in_q, place, me, seg, place)
        send(q_out.at[direct], q_in.at[seg, me], out_q, direct, me, other, direct)
    for place in near[1:]:
        send(q_out.at[place], q_in.at[seg, me], in_q, place, me, seg, place)

    def lines(which):
        st = st_in[which]
        centre = (
            lax.broadcasted_iota(jnp.int32, (n_ch, 1, LANES), 0) * s_dev
        ).astype(jnp.float32) + (mid_dev - mid_time)
        level = jnp.sum(st[:, 0:1, :], axis=0) / n_ch
        moment = s_dev * centre * st[:, 0:1, :] + spread_dev * st[:, 1:2, :]
        slope = jnp.sum(moment, axis=0) / spread
        return st, centre, level, slope

    def convert(which, level, slope, source, codes):
        wide = wide_here if which is seg else wide_there
        coef = st_in[which, source]
        centre = (source * s_dev).astype(jnp.float32) + (mid_dev - mid_time)
        first = coef[0:1] - level - slope * centre
        second = coef[1:2] - slope
        rest = codes.astype(jnp.int32).astype(jnp.float32) * coef[2:3]
        block = (rest + first + second * v_dev).astype(wide.dtype)
        for a in range(steps):
            row = L + source * s_dev - seg * lag_dev - a * SHIFTS
            rows = pl.ds(pl.multiple_of(row, SHIFTS), s_dev)
            wide[rows, a * c_dev : (a + 1) * c_dev] = block

    def arrive(sems, buf, k):
        remote(buf, buf, sems, k, k, seg, partner(1)).wait_recv()

    for k in z_ks:
        h = partner(k) // group
        arrive((z_send, z_recv), rq.at[seg, low, h], k // group)
        hop_refs(h, k // group)
    to_twin(0)
    for place in cross + near[1:]:
        arrive((s_send, s_recv), st_in.at[seg, place], place)
    send(st_in.at[seg], st_in.at[seg], (y_send, y_recv), 0, 0, other, me)
    _, _, level, slope = lines(seg)

    convert(seg, level, slope, me, q_out[me])
    for p, place in enumerate(cross):
        block = q_in.at[seg, place]
        arrive(in_q, block, place)
        send(block, block, out_q, place, place, other, me)
        convert(seg, level, slope, place, q_in[seg, place])
        if p == HOP_AT:
            for hop in range(1, len(hops)):
                j, x = hops[hop]
                for h in range(n_high):
                    row = partner(h * group) // group
                    block = rq.at[(seg + j) % 2, partner(x) % group, row]
                    arrive((x_send, x_recv), block, (hop - 1) * n_high + h)
                to_twin(hop)
    for place in near[1:]:
        arrive(in_q, q_in.at[seg, place], place)
        convert(seg, level, slope, place, q_in[seg, place])
    arrive((y_send, y_recv), st_in.at[other], 0)
    _, _, other_level, other_slope = lines(other)
    for place, (j, x) in enumerate(hops):
        arrive((t_send, t_recv), rq.at[(seg + j) % 2, partner(x + 1) % group], place)

    column_id = lax.broadcasted_iota(jnp.int32, (width, n_total), 1)
    is_left = lax.broadcasted_iota(jnp.int32, (half, LANES), 1) < s_dev
    lane = lax.broadcasted_iota(jnp.int32, (1, LANES), 1)
    time_id = lax.broadcasted_iota(jnp.int32, (n_ch, n_total), 1)
    in_part = time_id // s_dev == lax.broadcasted_iota(jnp.int32, (n_ch, n_total), 0)
    ones = in_part.astype(jnp.float32)
    ramps = jnp.where(in_part, (time_id % s_dev).astype(jnp.float32) - mid_dev, 0.0)
    patterns = jnp.concatenate([ones, ramps], axis=0)

    def shifted_refs(s, rt):
        st = [st_in[s, i] for i in range(n_ch)]
        centres = [i * s_dev + mid_dev - mid_time for i in range(n_ch)]
        both = sum(st[i][3:4] for i in range(n_ch))
        moved = sum(centres[i] * st[i][3:4] for i in range(n_ch))
        ref_stat = jnp.where(
            lane < width,
            both / n_ch,
            (s_dev * pltpu.roll(moved, width, 1) + spread_dev * both) / spread,
        )
        ref_slope = pltpu.roll(ref_stat, width, 1)
        first = jnp.concatenate(
            [
                st[i][3:4] - jnp.where(lane < width, ref_stat + centres[i] * ref_slope, ref_stat)
                for i in range(n_ch)
            ],
            axis=0,
        )
        scale = jnp.concatenate([st[i][4:5] for i in range(n_ch)], axis=0)
        coefs = jnp.concatenate([first, pltpu.roll(first, width, 1)], axis=0)

        def along(rows, pattern):
            return lax.dot_general(
                rows,
                pattern,
                (((0,), (0,)), ((), ())),
                precision=lax.Precision.HIGHEST,
                preferred_element_type=jnp.float32,
            )[:width]

        tops, lows = [], []
        for i in range(0, n_ch, 2):
            one = rq[s, i % group, i // group].astype(jnp.int32).astype(jnp.float32)
            two = rq[s, (i + 1) % group, (i + 1) // group].astype(jnp.int32).astype(jnp.float32)
            tops.append(jnp.where(is_left, one, pltpu.roll(two, s_dev, 1)))
            lows.append(jnp.where(is_left, pltpu.roll(one, s_dev, 1), two))
        series = jnp.concatenate(
            [jnp.concatenate(tops, axis=1), jnp.concatenate(lows, axis=1)], axis=0
        )
        series = series * along(scale, ones) + along(coefs, patterns)
        series = series.astype(rt.dtype)
        for b in range(SHIFTS):
            moved = series
            if b:
                moved = jnp.concatenate([jnp.zeros((width, b), rt.dtype), series[:, : n_total - b]], axis=1)
            rt[b * width : (b + 1) * width, :] = moved.astype(rt.dtype)

    quad = 4
    rows = quad * width

    def product(rt, wide, j):
        return jnp.dot(
            rt[j * rows : (j + 1) * rows, :],
            wide[L : L + n_total, :],
            preferred_element_type=jnp.float32,
        )

    shifted_refs(seg, rt_here)
    for j in range(SHIFTS // quad):
        acc[j] = product(rt_here, wide_here, j)
    shifted_refs(other, rt_there)
    for place in near:
        block = q_in.at[other, place]
        arrive(out_q, block, place)
        convert(other, other_level, other_slope, place, q_in[other, place])
    for place in cross:
        block = q_in.at[other, place]
        arrive(out_q, block, place)
        convert(other, other_level, other_slope, place, q_in[other, place])
    base = (seg * lag_dev).astype(jnp.float32)
    for j in range(SHIFTS // quad):
        total = acc[j] + product(rt_there, wide_there, j)
        for a in range(steps):
            for b in range(quad):
                k = a * SHIFTS + j * quad + b
                block = total[b * width : (b + 1) * width, a * c_dev : (a + 1) * c_dev]
                out_ref[k] = block * (1.0 / (2 * (n_total - (base + k))))
    for copy in sent:
        copy.wait_send()


def wide_blocks(strain, ref_local, owners):
    my_rows = strain[0]
    s_dev, chans = my_rows.shape
    n_ch = lax.axis_size("ch")
    n_seg = lax.axis_size("seg")
    n_total = s_dev * n_ch
    c_dev = chans // n_ch
    group = max(g for g in range(1, math.isqrt(n_ch) + 1) if n_ch % g == 0)
    n_high = n_ch // group
    width = ref_local.shape[0] * ref_local.shape[1]
    lag_dev = L // n_seg
    steps = lag_dev // SHIFTS
    picks = jnp.concatenate([ref_local, jnp.broadcast_to(owners[:, None], ref_local.shape)], axis=1)
    vmem = pl.BlockSpec(memory_space=pltpu.VMEM)
    dma = pltpu.SemaphoreType.DMA
    turned = pl.pallas_call(
        functools.partial(fused_kernel, n_ch, group, width),
        out_shape=jax.ShapeDtypeStruct((lag_dev, width, c_dev), jnp.float32),
        in_specs=[vmem, vmem],
        out_specs=vmem,
        scratch_shapes=[
            pltpu.SMEM(picks.shape, jnp.int32),
            pltpu.VMEM((n_ch, s_dev, c_dev), jnp.float32),
            pltpu.VMEM((n_ch, s_dev, c_dev), jnp.int16),
            pltpu.VMEM((n_ch, 5, c_dev), jnp.float32),
            pltpu.VMEM((n_seg, n_ch, s_dev, c_dev), jnp.int16),
            pltpu.VMEM((n_seg, n_ch, 5, c_dev), jnp.float32),
            pltpu.VMEM((n_seg, group, n_high, width // 2, LANES), jnp.int16),
            pltpu.VMEM((L + n_total, steps * c_dev), jnp.bfloat16),
            pltpu.VMEM((L + n_total, steps * c_dev), jnp.bfloat16),
            pltpu.VMEM((SHIFTS * width, n_total), jnp.bfloat16),
            pltpu.VMEM((SHIFTS * width, n_total), jnp.bfloat16),
            pltpu.VMEM((SHIFTS // 4, 4 * width, steps * c_dev), jnp.float32),
            dma((1,)),
            dma((n_ch,)), dma((n_ch,)),
            dma((n_seg, n_ch)), dma((n_seg, n_ch)),
            dma((n_high,)), dma((n_high,)),
            dma((n_seg * group * n_high,)), dma((n_seg * group * n_high,)),
            dma((n_seg * group,)), dma((n_seg * group,)),
            dma((1,)), dma((1,)),
        ],
        compiler_params=pltpu.CompilerParams(
            collective_id=0, has_side_effects=True, vmem_limit_bytes=GRANT
        ),
    )(my_rows, picks)
    return turned.transpose(0, 2, 1)


def solution(mesh):
    n_seg, n_ch = mesh.shape["seg"], mesh.shape["ch"]

    def per_device(strain, ref_local, owners):
        s_dev, chans = strain.shape[1:]
        fits = (
            chans == n_ch * LANES
            and n_seg == 2
            and (L // n_seg) % SHIFTS == 0
            and 2 * s_dev == LANES
            and n_ch >= 4
            and n_ch & (n_ch - 1) == 0
            and 2 * ref_local.size == LANES
        )
        return (wide_blocks if fits else narrow_blocks)(strain, ref_local, owners)

    in_specs = (P("seg", "ch", None), P(), P())
    out_specs = P("seg", "ch", None)
    return jax.shard_map(
        per_device, mesh=mesh, in_specs=in_specs, out_specs=out_specs, check_vma=False
    )
```

```python
import functools
import math

import jax
import jax.numpy as jnp
from jax import lax
from jax.experimental import pallas as pl
from jax.experimental.pallas import tpu as pltpu
from jax.sharding import PartitionSpec as P

L = 64
LANES = 128
SHIFTS = 16
GRANT = 24 * 1024 * 1024
STEPS = 32000.0
TINY = 1e-33
MESH = pl.DeviceIdType.MESH


def spread_2(block, axis, holder):
    block = jnp.where(lax.axis_index(axis) == holder, block, jnp.zeros_like(block))
    return lax.psum(block, axis)


def detrend_cols(series):
    n_total = series.shape[0]
    mid_time = (n_total - 1) / 2.0
    spread = n_total * (n_total * n_total - 1) / 12.0
    centred = (jnp.arange(n_total, dtype=jnp.float32) - mid_time)[:, None]
    level_val = jnp.sum(series, axis=0) / n_total
    slope_val = jnp.sum(centred * series, axis=0) / spread
    return (series - level_val - slope_val * centred).astype(jnp.bfloat16)


def owner_panels(detrended, ref_local, owners):
    pieces = []
    for panel_id in range(ref_local.shape[0]):
        own_cols = jnp.take(detrended, ref_local[panel_id], axis=1)
        pieces.append(spread_2(own_cols, "ch", owners[panel_id]))
    return jnp.concatenate(pieces, axis=1)


def narrow_blocks(strain, ref_local, owners):
    my_rows = strain[0]
    s_dev, chans = my_rows.shape
    n_ch = lax.axis_size("ch")
    n_seg = lax.axis_size("seg")
    n_total = s_dev * n_ch
    c_dev = chans // n_ch
    series = lax.all_to_all(my_rows, "ch", split_axis=1, concat_axis=0, tiled=True)
    detrended = detrend_cols(series)
    panels = owner_panels(detrended, ref_local, owners)
    width_ref = panels.shape[1]
    padded = jnp.concatenate([detrended, jnp.zeros((L, c_dev), jnp.bfloat16)], axis=0)
    blk_rows = min(512, n_total)
    n_blocks = n_total // blk_rows
    lag_dev = L // n_seg
    lag_count = lax.axis_size("seg") * lag_dev

    def add_block(blk_idx, running):
        blk_start = blk_idx * blk_rows
        window = lax.dynamic_slice_in_dim(padded, blk_start, blk_rows + lag_count - 1, 0)
        lagged = jnp.concatenate(
            [window[lag_off : lag_off + blk_rows] for lag_off in range(lag_count)], axis=1
        )
        ref_block = lax.dynamic_slice_in_dim(panels, blk_start, blk_rows, 0)
        return running + lax.dot_general(
            lagged, ref_block, (((0,), (0,)), ((), ())), preferred_element_type=jnp.float32
        )

    start_acc = jnp.zeros((lag_count * c_dev, width_ref), jnp.float32)
    running = lax.fori_loop(0, n_blocks, add_block, start_acc)
    summed = lax.psum_scatter(
        running.reshape(lag_count, c_dev, width_ref), "seg", scatter_dimension=0, tiled=True
    )
    lag_ids = (lax.axis_index("seg") * lag_dev + jnp.arange(lag_dev, dtype=jnp.int32)).astype(
        jnp.float32
    )
    return summed / (n_seg * (n_total - lag_ids))[:, None, None]


def fused_kernel(
    n_ch, group, width, strain_ref, picks_ref, out_ref,
    owners_ref, mine, q_out, st_out, q_in, st_in, rq, wide_here, wide_there, rt_here, rt_there, maps, acc,
    small_sem, s_send, s_recv, q_send, q_recv, z_send, z_recv,
    x_send, x_recv, t_send, t_recv, y_send, y_recv,
):
    seg = lax.axis_index("seg")
    me = lax.axis_index("ch")
    other = 1 - seg
    high, low = me // group, me % group
    n_high = n_ch // group
    s_dev = strain_ref.shape[0]
    c_dev = strain_ref.shape[1] // n_ch
    n_total = s_dev * n_ch
    n_panels = picks_ref.shape[0]
    panel_w = width // n_panels
    lag_dev = out_ref.shape[0]
    steps = lag_dev // SHIFTS
    mid_time = (n_total - 1) / 2.0
    spread = n_total * (n_total * n_total - 1) / 12.0
    mid_dev = (s_dev - 1) / 2.0
    spread_dev = s_dev * (s_dev * s_dev - 1) / 12.0
    half = width // 2
    upper = me // (n_ch // 2)

    def flip(place, k):
        bit = 1
        while bit <= k:
            if k & bit:
                place = place + (1 - 2 * ((me // bit) % 2)) * bit
            bit *= 2
        return place

    def partner(k):
        return flip(me, k)

    def far(p):
        row = (1 - upper) * (n_high // 2) + p // group
        return row * group + flip(low, p % group)

    near = [partner(k) for k in range(n_ch // 2)]
    cross = [far(p) for p in range(n_ch // 2)]

    def remote(src, dst, sems, k_send, k_recv, seg_to, ch_to):
        return pltpu.make_async_remote_copy(
            src_ref=src,
            dst_ref=dst,
            send_sem=sems[0].at[k_send],
            recv_sem=sems[1].at[k_recv],
            device_id=(seg_to, ch_to),
            device_id_type=MESH,
        )

    sent = []

    def send(*args):
        copy = remote(*args)
        copy.start()
        sent.append(copy)

    load_owners = pltpu.make_async_copy(picks_ref, owners_ref, small_sem.at[0])
    load_owners.start()
    barrier = pltpu.get_barrier_semaphore()
    for place in cross + near[1:]:
        pl.semaphore_signal(barrier, inc=1, device_id=(seg, place), device_id_type=MESH)
    for place in near:
        pl.semaphore_signal(barrier, inc=1, device_id=(other, place), device_id_type=MESH)

    for wide in (wide_here, wide_there):
        wide[n_total:, :] = jnp.zeros((L, steps * c_dev), wide.dtype)
    v_dev = lax.broadcasted_iota(jnp.int32, (s_dev, c_dev), 0).astype(jnp.float32) - mid_dev

    def code(block):
        v = v_dev[:, : block.shape[1]]
        level = jnp.sum(block, axis=0, keepdims=True) / s_dev
        slope = jnp.sum(v * block, axis=0, keepdims=True) / spread_dev
        rest = block - level - slope * v
        top = jnp.maximum(jnp.max(jnp.abs(rest), axis=0, keepdims=True), TINY)
        return level, slope, top / STEPS, jnp.round(rest * (STEPS / top))

    for o in range(n_ch):
        block = strain_ref[:, o * c_dev : (o + 1) * c_dev]
        mine[o] = block
        level, slope, scale, codes = code(block)
        q_out[o] = codes.astype(jnp.int32).astype(jnp.int16)
        st_out[o, 0:3, :] = jnp.concatenate([level, slope, scale], axis=0)

    load_owners.wait()
    blocks = jnp.concatenate(
        [mine[owners_ref[p, panel_w]] for p in range(n_panels)],
        axis=1,
    )
    targets = jnp.concatenate(
        [picks_ref[p : p + 1, :panel_w] + p * c_dev for p in range(n_panels)], axis=1
    )
    hot = (
        lax.broadcasted_iota(jnp.int32, (n_panels * c_dev, width), 0) == targets
    ).astype(jnp.float32)
    picked = jnp.dot(
        blocks, hot, precision=lax.Precision.HIGHEST, preferred_element_type=jnp.float32
    )
    level, slope, scale, codes = code(picked)
    ref_rows = jnp.concatenate(
        [jnp.concatenate([level, slope], axis=1), jnp.concatenate([scale, scale], axis=1)], axis=0
    )
    st_out[:, 3:5, :] = jnp.broadcast_to(ref_rows[None], (n_ch, 2, LANES))
    turned = codes.T
    rq[seg, low, high] = (
        jnp.concatenate([turned[:half], turned[half:]], axis=1)
        .astype(jnp.int32)
        .astype(jnp.int16)
    )
    st_in[seg, me] = st_out[me]

    pl.semaphore_wait(barrier, n_ch - 1 + len(near))

    hops = [(j, x) for j in range(2) for x in range(0, group, 2)]

    def hop_refs(h, k):
        block = rq.at[seg, low, h]
        for place, (j, x) in enumerate(hops[1:]):
            sem = place * n_high + k
            send(block, block, (x_send, x_recv), sem, sem, (seg + j) % 2, partner(x))

    def to_twin(place):
        j, x = hops[place]
        block = rq.at[(seg + j) % 2, partner(x) % group]
        send(block, block, (t_send, t_recv), place, place, seg, partner(1))

    z_ks = range(group, n_ch, group)
    for k in z_ks:
        block = rq.at[seg, low, high]
        send(block, block, (z_send, z_recv), k // group, k // group, seg, partner(k))
    hop_refs(high, 0)
    for place in cross + near[1:]:
        send(st_out.at[place], st_in.at[seg, me], (s_send, s_recv), place, me, seg, place)
    in_q = (q_send.at[0], q_recv.at[0])
    out_q = (q_send.at[1], q_recv.at[1])
    for place, direct in zip(cross, near):
        send(q_out.at[place], q_in.at[seg, me], in_q, place, me, seg, place)
        send(q_out.at[direct], q_in.at[seg, me], out_q, direct, me, other, direct)
    for place in near[1:]:
        send(q_out.at[place], q_in.at[seg, me], in_q, place, me, seg, place)

    def lines(which):
        st = st_in[which]
        centre = (
            lax.broadcasted_iota(jnp.int32, (n_ch, 1, LANES), 0) * s_dev
        ).astype(jnp.float32) + (mid_dev - mid_time)
        level = jnp.sum(st[:, 0:1, :], axis=0) / n_ch
        moment = s_dev * centre * st[:, 0:1, :] + spread_dev * st[:, 1:2, :]
        slope = jnp.sum(moment, axis=0) / spread
        return st, centre, level, slope

    def convert(which, level, slope, source, codes):
        wide = wide_here if which is seg else wide_there
        coef = st_in[which, source]
        centre = (source * s_dev).astype(jnp.float32) + (mid_dev - mid_time)
        first = coef[0:1] - level - slope * centre
        second = coef[1:2] - slope
        rest = codes.astype(jnp.int32).astype(jnp.float32) * coef[2:3]
        block = (rest + first + second * v_dev).astype(wide.dtype)
        for a in range(steps):
            row = L + source * s_dev - seg * lag_dev - a * SHIFTS
            rows = pl.ds(pl.multiple_of(row, SHIFTS), s_dev)
            wide[rows, a * c_dev : (a + 1) * c_dev] = block

    def arrive(sems, buf, k):
        remote(buf, buf, sems, k, k, seg, partner(1)).wait_recv()

    is_left = lax.broadcasted_iota(jnp.int32, (half, LANES), 1) < s_dev
    lane = lax.broadcasted_iota(jnp.int32, (1, LANES), 1)
    time_id = lax.broadcasted_iota(jnp.int32, (n_ch, n_total), 1)
    in_part = time_id // s_dev == lax.broadcasted_iota(jnp.int32, (n_ch, n_total), 0)
    ones = in_part.astype(jnp.float32)
    ramps = jnp.where(in_part, (time_id % s_dev).astype(jnp.float32) - mid_dev, 0.0)
    patterns = jnp.concatenate([ones, ramps], axis=0)

    def expand(s, plane):
        st = [st_in[s, i] for i in range(n_ch)]
        centres = [i * s_dev + mid_dev - mid_time for i in range(n_ch)]
        both = sum(st[i][3:4] for i in range(n_ch))
        moved = sum(centres[i] * st[i][3:4] for i in range(n_ch))
        ref_stat = jnp.where(
            lane < width,
            both / n_ch,
            (s_dev * pltpu.roll(moved, width, 1) + spread_dev * both) / spread,
        )
        ref_slope = pltpu.roll(ref_stat, width, 1)
        first = jnp.concatenate(
            [
                st[i][3:4] - jnp.where(lane < width, ref_stat + centres[i] * ref_slope, ref_stat)
                for i in range(n_ch)
            ],
            axis=0,
        )
        scale = jnp.concatenate([st[i][4:5] for i in range(n_ch)], axis=0)
        coefs = jnp.concatenate([first, pltpu.roll(first, width, 1)], axis=0)

        def along(rows, pattern):
            return lax.dot_general(
                rows,
                pattern,
                (((0,), (0,)), ((), ())),
                precision=lax.Precision.HIGHEST,
                preferred_element_type=jnp.float32,
            )[:width]

        maps[plane, 0] = along(scale, ones)
        maps[plane, 1] = along(coefs, patterns)

    def ref_series(s, plane):
        tops, lows = [], []
        for i in range(0, n_ch, 2):
            one = rq[s, i % group, i // group].astype(jnp.int32).astype(jnp.float32)
            two = rq[s, (i + 1) % group, (i + 1) // group].astype(jnp.int32).astype(jnp.float32)
            tops.append(jnp.where(is_left, one, pltpu.roll(two, s_dev, 1)))
            lows.append(jnp.where(is_left, pltpu.roll(one, s_dev, 1), two))
        series = jnp.concatenate(
            [jnp.concatenate(tops, axis=1), jnp.concatenate(lows, axis=1)], axis=0
        )
        return (series * maps[plane, 0] + maps[plane, 1]).astype(rt_here.dtype)

    def shift_refs(series, rt, b):
        moved = series
        if b:
            blank = jnp.zeros((width, b), rt.dtype)
            moved = jnp.concatenate([blank, series[:, : n_total - b]], axis=1)
        rt[b * width : (b + 1) * width, :] = moved

    def hop_far_refs():
        for k in z_ks:
            h = partner(k) // group
            arrive((z_send, z_recv), rq.at[seg, low, h], k // group)
            hop_refs(h, k // group)
        to_twin(0)

    def take_lines():
        for place in cross + near[1:]:
            arrive((s_send, s_recv), st_in.at[seg, place], place)
        send(st_in.at[seg], st_in.at[seg], (y_send, y_recv), 0, 0, other, me)
        return lines(seg)[2:]

    def hand_over(places):
        for place in places:
            block = q_in.at[seg, place]
            arrive(in_q, block, place)
            send(block, block, out_q, place, place, other, me)

    def pass_to_twin():
        for hop in range(1, len(hops)):
            j, x = hops[hop]
            for h in range(n_high):
                row = partner(h * group) // group
                block = rq.at[(seg + j) % 2, partner(x) % group, row]
                arrive((x_send, x_recv), block, (hop - 1) * n_high + h)
            to_twin(hop)

    def convert_here(places):
        for place in places:
            convert(seg, level, slope, place, q_in[seg, place])

    hop_far_refs()
    level, slope = take_lines()
    expand(seg, 0)
    convert(seg, level, slope, me, q_out[me])
    hand_over(cross[0:1])
    convert_here(cross[0:1])
    hand_over(cross[1:2])
    convert_here(cross[1:2])
    hand_over(cross[2:3])
    convert_here(cross[2:3])
    hand_over(cross[3:4])
    convert_here(cross[3:4])
    hand_over(cross[4:5])
    convert_here(cross[4:5])
    hand_over(cross[5:6])
    convert_here(cross[5:6])
    pass_to_twin()
    hand_over(cross[6:7])
    convert_here(cross[6:7])
    hand_over(cross[7:8])
    convert_here(cross[7:8])
    for place in near[1:]:
        arrive(in_q, q_in.at[seg, place], place)
        convert(seg, level, slope, place, q_in[seg, place])
    arrive((y_send, y_recv), st_in.at[other], 0)
    _, _, other_level, other_slope = lines(other)
    expand(other, 1)
    for place in near:
        block = q_in.at[other, place]
        arrive(out_q, block, place)
        convert(other, other_level, other_slope, place, q_in[other, place])
    for place, (j, x) in enumerate(hops):
        arrive((t_send, t_recv), rq.at[(seg + j) % 2, partner(x + 1) % group], place)

    quad = 4
    rows = quad * width

    def product(rt, wide, j):
        return jnp.dot(
            rt[j * rows : (j + 1) * rows, :],
            wide[L : L + n_total, :],
            preferred_element_type=jnp.float32,
        )

    series = ref_series(seg, 0)
    for b in range(SHIFTS):
        shift_refs(series, rt_here, b)
    series = ref_series(other, 1)
    for j in range(SHIFTS // quad):
        acc[j] = product(rt_here, wide_here, j)
        for b in range(j * quad, (j + 1) * quad):
            shift_refs(series, rt_there, b)
    for place in cross:
        block = q_in.at[other, place]
        arrive(out_q, block, place)
        convert(other, other_level, other_slope, place, q_in[other, place])
    base = (seg * lag_dev).astype(jnp.float32)
    for j in range(SHIFTS // quad):
        total = acc[j] + product(rt_there, wide_there, j)
        for a in range(steps):
            for b in range(quad):
                k = a * SHIFTS + j * quad + b
                block = total[b * width : (b + 1) * width, a * c_dev : (a + 1) * c_dev]
                out_ref[k] = block * (1.0 / (2 * (n_total - (base + k))))
    for copy in sent:
        copy.wait_send()


def wide_blocks(strain, ref_local, owners):
    my_rows = strain[0]
    s_dev, chans = my_rows.shape
    n_ch = lax.axis_size("ch")
    n_seg = lax.axis_size("seg")
    n_total = s_dev * n_ch
    c_dev = chans // n_ch
    group = max(g for g in range(1, math.isqrt(n_ch) + 1) if n_ch % g == 0)
    n_high = n_ch // group
    width = ref_local.shape[0] * ref_local.shape[1]
    lag_dev = L // n_seg
    steps = lag_dev // SHIFTS
    picks = jnp.concatenate([ref_local, owners[:, None]], axis=1)
    vmem = pl.BlockSpec(memory_space=pltpu.VMEM)
    dma = pltpu.SemaphoreType.DMA
    turned = pl.pallas_call(
        functools.partial(fused_kernel, n_ch, group, width),
        out_shape=jax.ShapeDtypeStruct((lag_dev, width, c_dev), jnp.float32),
        in_specs=[vmem, vmem],
        out_specs=vmem,
        scratch_shapes=[
            pltpu.SMEM(picks.shape, jnp.int32),
            pltpu.VMEM((n_ch, s_dev, c_dev), jnp.float32),
            pltpu.VMEM((n_ch, s_dev, c_dev), jnp.int16),
            pltpu.VMEM((n_ch, 5, c_dev), jnp.float32),
            pltpu.VMEM((n_seg, n_ch, s_dev, c_dev), jnp.int16),
            pltpu.VMEM((n_seg, n_ch, 5, c_dev), jnp.float32),
            pltpu.VMEM((n_seg, group, n_high, width // 2, LANES), jnp.int16),
            pltpu.VMEM((L + n_total, steps * c_dev), jnp.bfloat16),
            pltpu.VMEM((L + n_total, steps * c_dev), jnp.bfloat16),
            pltpu.VMEM((SHIFTS * width, n_total), jnp.bfloat16),
            pltpu.VMEM((SHIFTS * width, n_total), jnp.bfloat16),
            pltpu.VMEM((n_seg, 2, width, n_total), jnp.float32),
            pltpu.VMEM((SHIFTS // 4, 4 * width, steps * c_dev), jnp.float32),
            dma((1,)),
            dma((n_ch,)), dma((n_ch,)),
            dma((n_seg, n_ch)), dma((n_seg, n_ch)),
            dma((n_high,)), dma((n_high,)),
            dma((n_seg * group * n_high,)), dma((n_seg * group * n_high,)),
            dma((n_seg * group,)), dma((n_seg * group,)),
            dma((1,)), dma((1,)),
        ],
        compiler_params=pltpu.CompilerParams(
            collective_id=0, has_side_effects=True, vmem_limit_bytes=GRANT
        ),
    )(my_rows, picks)
    return turned.transpose(0, 2, 1)


def solution(mesh):
    n_seg, n_ch = mesh.shape["seg"], mesh.shape["ch"]

    def per_device(strain, ref_local, owners):
        s_dev, chans = strain.shape[1:]
        fits = (
            chans == n_ch * LANES
            and n_seg == 2
            and (L // n_seg) % SHIFTS == 0
            and 2 * s_dev == LANES
            and n_ch >= 4
            and n_ch & (n_ch - 1) == 0
            and 2 * ref_local.size == LANES
        )
        return (wide_blocks if fits else narrow_blocks)(strain, ref_local, owners)

    in_specs = (P("seg", "ch", None), P(), P())
    out_specs = P("seg", "ch", None)
    return jax.shard_map(
        per_device, mesh=mesh, in_specs=in_specs, out_specs=out_specs, check_vma=False
    )
```

```python
import functools
import math

import jax
import jax.numpy as jnp
from jax import lax
from jax.experimental import pallas as pl
from jax.experimental.pallas import tpu as pltpu
from jax.sharding import PartitionSpec as P

L = 64
LANES = 128
SHIFTS = 16
GRANT = 24 * 1024 * 1024
STEPS = 32000.0
TINY = 1e-33
MESH = pl.DeviceIdType.MESH


def spread_2(block, axis, holder):
    block = jnp.where(lax.axis_index(axis) == holder, block, jnp.zeros_like(block))
    return lax.psum(block, axis)


def detrend_cols(series):
    n_total = series.shape[0]
    mid_time = (n_total - 1) / 2.0
    spread = n_total * (n_total * n_total - 1) / 12.0
    centred = (jnp.arange(n_total, dtype=jnp.float32) - mid_time)[:, None]
    level_val = jnp.sum(series, axis=0) / n_total
    slope_val = jnp.sum(centred * series, axis=0) / spread
    return (series - level_val - slope_val * centred).astype(jnp.bfloat16)


def owner_panels(detrended, ref_local, owners):
    pieces = []
    for panel_id in range(ref_local.shape[0]):
        own_cols = jnp.take(detrended, ref_local[panel_id], axis=1)
        pieces.append(spread_2(own_cols, "ch", owners[panel_id]))
    return jnp.concatenate(pieces, axis=1)


def narrow_blocks(strain, ref_local, owners):
    my_rows = strain[0]
    s_dev, chans = my_rows.shape
    n_ch = lax.axis_size("ch")
    n_seg = lax.axis_size("seg")
    n_total = s_dev * n_ch
    c_dev = chans // n_ch
    series = lax.all_to_all(my_rows, "ch", split_axis=1, concat_axis=0, tiled=True)
    detrended = detrend_cols(series)
    panels = owner_panels(detrended, ref_local, owners)
    width_ref = panels.shape[1]
    padded = jnp.concatenate([detrended, jnp.zeros((L, c_dev), jnp.bfloat16)], axis=0)
    blk_rows = min(512, n_total)
    n_blocks = n_total // blk_rows
    lag_dev = L // n_seg
    lag_count = lax.axis_size("seg") * lag_dev

    def add_block(blk_idx, running):
        blk_start = blk_idx * blk_rows
        window = lax.dynamic_slice_in_dim(padded, blk_start, blk_rows + lag_count - 1, 0)
        lagged = jnp.concatenate(
            [window[lag_off : lag_off + blk_rows] for lag_off in range(lag_count)], axis=1
        )
        ref_block = lax.dynamic_slice_in_dim(panels, blk_start, blk_rows, 0)
        return running + lax.dot_general(
            lagged, ref_block, (((0,), (0,)), ((), ())), preferred_element_type=jnp.float32
        )

    start_acc = jnp.zeros((lag_count * c_dev, width_ref), jnp.float32)
    running = lax.fori_loop(0, n_blocks, add_block, start_acc)
    summed = lax.psum_scatter(
        running.reshape(lag_count, c_dev, width_ref), "seg", scatter_dimension=0, tiled=True
    )
    lag_ids = (lax.axis_index("seg") * lag_dev + jnp.arange(lag_dev, dtype=jnp.int32)).astype(
        jnp.float32
    )
    return summed / (n_seg * (n_total - lag_ids))[:, None, None]


def fused_kernel(
    n_ch, group, width, strain_ref, picks_ref, out_ref,
    owners_ref, mine, q_out, st_out, q_in, st_in, rq, wide_here, wide_there, rt_here, rt_there, maps, acc,
    small_sem, s_send, s_recv, q_send, q_recv, z_send, z_recv,
    x_send, x_recv, t_send, t_recv, y_send, y_recv,
):
    seg = lax.axis_index("seg")
    me = lax.axis_index("ch")
    other = 1 - seg
    high, low = me // group, me % group
    n_high = n_ch // group
    s_dev = strain_ref.shape[0]
    c_dev = strain_ref.shape[1] // n_ch
    n_total = s_dev * n_ch
    n_panels = picks_ref.shape[0]
    panel_w = width // n_panels
    lag_dev = out_ref.shape[0]
    steps = lag_dev // SHIFTS
    mid_time = (n_total - 1) / 2.0
    spread = n_total * (n_total * n_total - 1) / 12.0
    mid_dev = (s_dev - 1) / 2.0
    spread_dev = s_dev * (s_dev * s_dev - 1) / 12.0
    half = width // 2
    upper = me // (n_ch // 2)

    def flip(place, k):
        bit = 1
        while bit <= k:
            if k & bit:
                place = place + (1 - 2 * ((me // bit) % 2)) * bit
            bit *= 2
        return place

    def partner(k):
        return flip(me, k)

    def far(p):
        row = (1 - upper) * (n_high // 2) + p // group
        place = p % group
        return row * group + place // 2 * 2 + (me + place) % 2

    near = [partner(k) for k in range(n_ch // 2)]
    cross = [far(p) for p in range(n_ch // 2)]

    def remote(src, dst, sems, k_send, k_recv, seg_to, ch_to):
        return pltpu.make_async_remote_copy(
            src_ref=src,
            dst_ref=dst,
            send_sem=sems[0].at[k_send],
            recv_sem=sems[1].at[k_recv],
            device_id=(seg_to, ch_to),
            device_id_type=MESH,
        )

    sent = []

    def send(*args):
        copy = remote(*args)
        copy.start()
        sent.append(copy)

    load_owners = pltpu.make_async_copy(picks_ref, owners_ref, small_sem.at[0])
    load_owners.start()
    barrier = pltpu.get_barrier_semaphore()
    for place in cross + near[1:]:
        pl.semaphore_signal(barrier, inc=1, device_id=(seg, place), device_id_type=MESH)
    for place in near:
        pl.semaphore_signal(barrier, inc=1, device_id=(other, place), device_id_type=MESH)

    for wide in (wide_here, wide_there):
        wide[n_total:, :] = jnp.zeros((L, steps * c_dev), wide.dtype)
    v_dev = lax.broadcasted_iota(jnp.int32, (s_dev, c_dev), 0).astype(jnp.float32) - mid_dev

    def code(block):
        v = v_dev[:, : block.shape[1]]
        level = jnp.sum(block, axis=0, keepdims=True) / s_dev
        slope = jnp.sum(v * block, axis=0, keepdims=True) / spread_dev
        rest = block - level - slope * v
        top = jnp.maximum(jnp.max(jnp.abs(rest), axis=0, keepdims=True), TINY)
        return level, slope, top / STEPS, jnp.round(rest * (STEPS / top))

    for o in range(n_ch):
        block = strain_ref[:, o * c_dev : (o + 1) * c_dev]
        mine[o] = block
        level, slope, scale, codes = code(block)
        q_out[o] = codes.astype(jnp.int32).astype(jnp.int16)
        st_out[o, 0:3, :] = jnp.concatenate([level, slope, scale], axis=0)

    load_owners.wait()
    blocks = jnp.concatenate(
        [mine[owners_ref[p, panel_w]] for p in range(n_panels)],
        axis=1,
    )
    targets = jnp.concatenate(
        [picks_ref[p : p + 1, :panel_w] + p * c_dev for p in range(n_panels)], axis=1
    )
    hot = (
        lax.broadcasted_iota(jnp.int32, (n_panels * c_dev, width), 0) == targets
    ).astype(jnp.float32)
    picked = jnp.dot(
        blocks, hot, precision=lax.Precision.HIGHEST, preferred_element_type=jnp.float32
    )
    level, slope, scale, codes = code(picked)
    ref_rows = jnp.concatenate(
        [jnp.concatenate([level, slope], axis=1), jnp.concatenate([scale, scale], axis=1)], axis=0
    )
    st_out[:, 3:5, :] = jnp.broadcast_to(ref_rows[None], (n_ch, 2, LANES))
    turned = codes.T
    rq[seg, low, high] = (
        jnp.concatenate([turned[:half], turned[half:]], axis=1)
        .astype(jnp.int32)
        .astype(jnp.int16)
    )
    st_in[seg, me] = st_out[me]

    pl.semaphore_wait(barrier, n_ch - 1 + len(near))

    hops = [(j, x) for j in range(2) for x in range(0, group, 2)]

    def hop_refs(h, k):
        block = rq.at[seg, low, h]
        for place, (j, x) in enumerate(hops[1:]):
            sem = place * n_high + k
            send(block, block, (x_send, x_recv), sem, sem, (seg + j) % 2, partner(x))

    def to_twin(place):
        j, x = hops[place]
        block = rq.at[(seg + j) % 2, partner(x) % group]
        send(block, block, (t_send, t_recv), place, place, seg, partner(1))

    z_ks = range(group, n_ch, group)
    for k in z_ks:
        block = rq.at[seg, low, high]
        send(block, block, (z_send, z_recv), k // group, k // group, seg, partner(k))
    hop_refs(high, 0)
    for place in cross + near[1:]:
        send(st_out.at[place], st_in.at[seg, me], (s_send, s_recv), place, me, seg, place)
    in_q = (q_send.at[0], q_recv.at[0])
    out_q = (q_send.at[1], q_recv.at[1])
    for place, direct in zip(cross, near[n_ch // 4 :] + near[: n_ch // 4]):
        send(q_out.at[place], q_in.at[seg, me], in_q, place, me, seg, place)
        send(q_out.at[direct], q_in.at[seg, me], out_q, direct, me, other, direct)
    for place in near[1:]:
        send(q_out.at[place], q_in.at[seg, me], in_q, place, me, seg, place)

    def lines(which):
        st = st_in[which]
        centre = (
            lax.broadcasted_iota(jnp.int32, (n_ch, 1, LANES), 0) * s_dev
        ).astype(jnp.float32) + (mid_dev - mid_time)
        level = jnp.sum(st[:, 0:1, :], axis=0) / n_ch
        moment = s_dev * centre * st[:, 0:1, :] + spread_dev * st[:, 1:2, :]
        slope = jnp.sum(moment, axis=0) / spread
        return st, centre, level, slope

    def convert(which, level, slope, source, codes):
        wide = wide_here if which is seg else wide_there
        coef = st_in[which, source]
        centre = (source * s_dev).astype(jnp.float32) + (mid_dev - mid_time)
        first = coef[0:1] - level - slope * centre
        second = coef[1:2] - slope
        rest = codes.astype(jnp.int32).astype(jnp.float32) * coef[2:3]
        block = (rest + first + second * v_dev).astype(wide.dtype)
        for a in range(steps):
            row = L + source * s_dev - seg * lag_dev - a * SHIFTS
            rows = pl.ds(pl.multiple_of(row, SHIFTS), s_dev)
            wide[rows, a * c_dev : (a + 1) * c_dev] = block

    def arrive(sems, buf, k):
        remote(buf, buf, sems, k, k, seg, partner(1)).wait_recv()

    is_left = lax.broadcasted_iota(jnp.int32, (half, LANES), 1) < s_dev
    lane = lax.broadcasted_iota(jnp.int32, (1, LANES), 1)
    time_id = lax.broadcasted_iota(jnp.int32, (n_ch, n_total), 1)
    in_part = time_id // s_dev == lax.broadcasted_iota(jnp.int32, (n_ch, n_total), 0)
    ones = in_part.astype(jnp.float32)
    ramps = jnp.where(in_part, (time_id % s_dev).astype(jnp.float32) - mid_dev, 0.0)
    patterns = jnp.concatenate([ones, ramps], axis=0)

    def expand(s, plane):
        st = [st_in[s, i] for i in range(n_ch)]
        centres = [i * s_dev + mid_dev - mid_time for i in range(n_ch)]
        both = sum(st[i][3:4] for i in range(n_ch))
        moved = sum(centres[i] * st[i][3:4] for i in range(n_ch))
        ref_stat = jnp.where(
            lane < width,
            both / n_ch,
            (s_dev * pltpu.roll(moved, width, 1) + spread_dev * both) / spread,
        )
        ref_slope = pltpu.roll(ref_stat, width, 1)
        first = jnp.concatenate(
            [
                st[i][3:4] - jnp.where(lane < width, ref_stat + centres[i] * ref_slope, ref_stat)
                for i in range(n_ch)
            ],
            axis=0,
        )
        scale = jnp.concatenate([st[i][4:5] for i in range(n_ch)], axis=0)
        coefs = jnp.concatenate([first, pltpu.roll(first, width, 1)], axis=0)

        def along(rows, pattern):
            return lax.dot_general(
                rows,
                pattern,
                (((0,), (0,)), ((), ())),
                precision=lax.Precision.HIGHEST,
                preferred_element_type=jnp.float32,
            )[:width]

        maps[plane, 0] = along(scale, ones)
        maps[plane, 1] = along(coefs, patterns)

    def ref_series(s, plane):
        tops, lows = [], []
        for i in range(0, n_ch, 2):
            one = rq[s, i % group, i // group].astype(jnp.int32).astype(jnp.float32)
            two = rq[s, (i + 1) % group, (i + 1) // group].astype(jnp.int32).astype(jnp.float32)
            tops.append(jnp.where(is_left, one, pltpu.roll(two, s_dev, 1)))
            lows.append(jnp.where(is_left, pltpu.roll(one, s_dev, 1), two))
        series = jnp.concatenate(
            [jnp.concatenate(tops, axis=1), jnp.concatenate(lows, axis=1)], axis=0
        )
        return (series * maps[plane, 0] + maps[plane, 1]).astype(rt_here.dtype)

    def shift_refs(series, rt, b):
        moved = series
        if b:
            blank = jnp.zeros((width, b), rt.dtype)
            moved = jnp.concatenate([blank, series[:, : n_total - b]], axis=1)
        rt[b * width : (b + 1) * width, :] = moved

    def hop_far_refs():
        for k in z_ks:
            h = partner(k) // group
            arrive((z_send, z_recv), rq.at[seg, low, h], k // group)
            hop_refs(h, k // group)
        to_twin(0)

    def take_lines():
        for place in cross + near[1:]:
            arrive((s_send, s_recv), st_in.at[seg, place], place)
        send(st_in.at[seg], st_in.at[seg], (y_send, y_recv), 0, 0, other, me)
        return lines(seg)[2:]

    def hand_over(places):
        for place in places:
            block = q_in.at[seg, place]
            arrive(in_q, block, place)
            send(block, block, out_q, place, place, other, me)

    def pass_to_twin():
        for hop in range(1, len(hops)):
            j, x = hops[hop]
            for h in range(n_high):
                row = partner(h * group) // group
                block = rq.at[(seg + j) % 2, partner(x) % group, row]
                arrive((x_send, x_recv), block, (hop - 1) * n_high + h)
            to_twin(hop)

    def convert_here(places):
        for place in places:
            convert(seg, level, slope, place, q_in[seg, place])

    hop_far_refs()
    level, slope = take_lines()
    expand(seg, 0)
    convert(seg, level, slope, me, q_out[me])
    hand_over(cross[0:1])
    convert_here(cross[0:1])
    hand_over(cross[1:2])
    convert_here(cross[1:2])
    hand_over(cross[2:3])
    convert_here(cross[2:3])
    hand_over(cross[3:4])
    convert_here(cross[3:4])
    hand_over(cross[4:5])
    convert_here(cross[4:5])
    hand_over(cross[5:6])
    convert_here(cross[5:6])
    pass_to_twin()
    hand_over(cross[6:7])
    convert_here(cross[6:7])
    hand_over(cross[7:8])
    convert_here(cross[7:8])
    for place in near[1:]:
        arrive(in_q, q_in.at[seg, place], place)
        convert(seg, level, slope, place, q_in[seg, place])
    arrive((y_send, y_recv), st_in.at[other], 0)
    _, _, other_level, other_slope = lines(other)
    expand(other, 1)
    for place in near:
        block = q_in.at[other, place]
        arrive(out_q, block, place)
        convert(other, other_level, other_slope, place, q_in[other, place])
    for place, (j, x) in enumerate(hops):
        arrive((t_send, t_recv), rq.at[(seg + j) % 2, partner(x + 1) % group], place)

    quad = 4
    rows = quad * width

    def product(rt, wide, j):
        return jnp.dot(
            rt[j * rows : (j + 1) * rows, :],
            wide[L : L + n_total, :],
            preferred_element_type=jnp.float32,
        )

    series = ref_series(seg, 0)
    for b in range(SHIFTS):
        shift_refs(series, rt_here, b)
    series = ref_series(other, 1)
    for j in range(SHIFTS // quad):
        acc[j] = product(rt_here, wide_here, j)
        for b in range(j * quad, (j + 1) * quad):
            shift_refs(series, rt_there, b)
    for place in cross:
        block = q_in.at[other, place]
        arrive(out_q, block, place)
        convert(other, other_level, other_slope, place, q_in[other, place])
    base = (seg * lag_dev).astype(jnp.float32)
    for j in range(SHIFTS // quad):
        total = acc[j] + product(rt_there, wide_there, j)
        for a in range(steps):
            for b in range(quad):
                k = a * SHIFTS + j * quad + b
                block = total[b * width : (b + 1) * width, a * c_dev : (a + 1) * c_dev]
                out_ref[k] = block * (1.0 / (2 * (n_total - (base + k))))
    for copy in sent:
        copy.wait_send()


def wide_blocks(strain, ref_local, owners):
    my_rows = strain[0]
    s_dev, chans = my_rows.shape
    n_ch = lax.axis_size("ch")
    n_seg = lax.axis_size("seg")
    n_total = s_dev * n_ch
    c_dev = chans // n_ch
    group = max(g for g in range(1, math.isqrt(n_ch) + 1) if n_ch % g == 0)
    n_high = n_ch // group
    width = ref_local.shape[0] * ref_local.shape[1]
    lag_dev = L // n_seg
    steps = lag_dev // SHIFTS
    picks = jnp.concatenate([ref_local, owners[:, None]], axis=1)
    vmem = pl.BlockSpec(memory_space=pltpu.VMEM)
    dma = pltpu.SemaphoreType.DMA
    turned = pl.pallas_call(
        functools.partial(fused_kernel, n_ch, group, width),
        out_shape=jax.ShapeDtypeStruct((lag_dev, width, c_dev), jnp.float32),
        in_specs=[vmem, vmem],
        out_specs=vmem,
        scratch_shapes=[
            pltpu.SMEM(picks.shape, jnp.int32),
            pltpu.VMEM((n_ch, s_dev, c_dev), jnp.float32),
            pltpu.VMEM((n_ch, s_dev, c_dev), jnp.int16),
            pltpu.VMEM((n_ch, 5, c_dev), jnp.float32),
            pltpu.VMEM((n_seg, n_ch, s_dev, c_dev), jnp.int16),
            pltpu.VMEM((n_seg, n_ch, 5, c_dev), jnp.float32),
            pltpu.VMEM((n_seg, group, n_high, width // 2, LANES), jnp.int16),
            pltpu.VMEM((L + n_total, steps * c_dev), jnp.bfloat16),
            pltpu.VMEM((L + n_total, steps * c_dev), jnp.bfloat16),
            pltpu.VMEM((SHIFTS * width, n_total), jnp.bfloat16),
            pltpu.VMEM((SHIFTS * width, n_total), jnp.bfloat16),
            pltpu.VMEM((n_seg, 2, width, n_total), jnp.float32),
            pltpu.VMEM((SHIFTS // 4, 4 * width, steps * c_dev), jnp.float32),
            dma((1,)),
            dma((n_ch,)), dma((n_ch,)),
            dma((n_seg, n_ch)), dma((n_seg, n_ch)),
            dma((n_high,)), dma((n_high,)),
            dma((n_seg * group * n_high,)), dma((n_seg * group * n_high,)),
            dma((n_seg * group,)), dma((n_seg * group,)),
            dma((1,)), dma((1,)),
        ],
        compiler_params=pltpu.CompilerParams(
            collective_id=0, has_side_effects=True, vmem_limit_bytes=GRANT
        ),
    )(my_rows, picks)
    return turned.transpose(0, 2, 1)


def solution(mesh):
    n_seg, n_ch = mesh.shape["seg"], mesh.shape["ch"]

    def per_device(strain, ref_local, owners):
        s_dev, chans = strain.shape[1:]
        fits = (
            chans == n_ch * LANES
            and n_seg == 2
            and (L // n_seg) % SHIFTS == 0
            and 2 * s_dev == LANES
            and n_ch >= 4
            and n_ch & (n_ch - 1) == 0
            and 2 * ref_local.size == LANES
        )
        return (wide_blocks if fits else narrow_blocks)(strain, ref_local, owners)

    in_specs = (P("seg", "ch", None), P(), P())
    out_specs = P("seg", "ch", None)
    return jax.shard_map(
        per_device, mesh=mesh, in_specs=in_specs, out_specs=out_specs, check_vma=False
    )
```

```python
import functools
import math

import jax
import jax.numpy as jnp
from jax import lax
from jax.experimental import pallas as pl
from jax.experimental.pallas import tpu as pltpu
from jax.sharding import PartitionSpec as P

L = 64
LANES = 128
SHIFTS = 16
GRANT = 24 * 1024 * 1024
STEPS = 32000.0
TINY = 1e-33
MESH = pl.DeviceIdType.MESH


def spread_2(block, axis, holder):
    block = jnp.where(lax.axis_index(axis) == holder, block, jnp.zeros_like(block))
    return lax.psum(block, axis)


def detrend_cols(series):
    n_total = series.shape[0]
    mid_time = (n_total - 1) / 2.0
    spread = n_total * (n_total * n_total - 1) / 12.0
    centred = (jnp.arange(n_total, dtype=jnp.float32) - mid_time)[:, None]
    level_val = jnp.sum(series, axis=0) / n_total
    slope_val = jnp.sum(centred * series, axis=0) / spread
    return (series - level_val - slope_val * centred).astype(jnp.bfloat16)


def owner_panels(detrended, ref_local, owners):
    pieces = []
    for panel_id in range(ref_local.shape[0]):
        own_cols = jnp.take(detrended, ref_local[panel_id], axis=1)
        pieces.append(spread_2(own_cols, "ch", owners[panel_id]))
    return jnp.concatenate(pieces, axis=1)


def narrow_blocks(strain, ref_local, owners):
    my_rows = strain[0]
    s_dev, chans = my_rows.shape
    n_ch = lax.axis_size("ch")
    n_seg = lax.axis_size("seg")
    n_total = s_dev * n_ch
    c_dev = chans // n_ch
    series = lax.all_to_all(my_rows, "ch", split_axis=1, concat_axis=0, tiled=True)
    detrended = detrend_cols(series)
    panels = owner_panels(detrended, ref_local, owners)
    width_ref = panels.shape[1]
    padded = jnp.concatenate([detrended, jnp.zeros((L, c_dev), jnp.bfloat16)], axis=0)
    blk_rows = min(512, n_total)
    n_blocks = n_total // blk_rows
    lag_dev = L // n_seg
    lag_count = lax.axis_size("seg") * lag_dev

    def add_block(blk_idx, running):
        blk_start = blk_idx * blk_rows
        window = lax.dynamic_slice_in_dim(padded, blk_start, blk_rows + lag_count - 1, 0)
        lagged = jnp.concatenate(
            [window[lag_off : lag_off + blk_rows] for lag_off in range(lag_count)], axis=1
        )
        ref_block = lax.dynamic_slice_in_dim(panels, blk_start, blk_rows, 0)
        return running + lax.dot_general(
            lagged, ref_block, (((0,), (0,)), ((), ())), preferred_element_type=jnp.float32
        )

    start_acc = jnp.zeros((lag_count * c_dev, width_ref), jnp.float32)
    running = lax.fori_loop(0, n_blocks, add_block, start_acc)
    summed = lax.psum_scatter(
        running.reshape(lag_count, c_dev, width_ref), "seg", scatter_dimension=0, tiled=True
    )
    lag_ids = (lax.axis_index("seg") * lag_dev + jnp.arange(lag_dev, dtype=jnp.int32)).astype(
        jnp.float32
    )
    return summed / (n_seg * (n_total - lag_ids))[:, None, None]


def fused_kernel(
    n_ch, group, width, strain_ref, picks_ref, out_ref,
    owners_ref, mine, q_out, st_out, q_in, st_in, rq, wide_here, wide_there, rt_here, rt_there, maps, acc,
    small_sem, s_send, s_recv, q_send, q_recv, z_send, z_recv,
    x_send, x_recv, t_send, t_recv, y_send, y_recv,
):
    seg = lax.axis_index("seg")
    me = lax.axis_index("ch")
    other = 1 - seg
    high, low = me // group, me % group
    n_high = n_ch // group
    s_dev = strain_ref.shape[0]
    c_dev = strain_ref.shape[1] // n_ch
    n_total = s_dev * n_ch
    n_panels = picks_ref.shape[0] - 1
    panel_w = width // n_panels
    lag_dev = out_ref.shape[0]
    steps = lag_dev // SHIFTS
    mid_time = (n_total - 1) / 2.0
    spread = n_total * (n_total * n_total - 1) / 12.0
    mid_dev = (s_dev - 1) / 2.0
    spread_dev = s_dev * (s_dev * s_dev - 1) / 12.0
    half = width // 2
    upper = me // (n_ch // 2)

    def flip(place, k):
        bit = 1
        while bit <= k:
            if k & bit:
                place = place + (1 - 2 * ((me // bit) % 2)) * bit
            bit *= 2
        return place

    def partner(k):
        return flip(me, k)

    def far(p):
        row = (1 - upper) * (n_high // 2) + p // group
        place = p % group
        return row * group + place // 2 * 2 + (me + place) % 2

    near = [partner(k) for k in range(n_ch // 2)]
    cross = [far(p) for p in range(n_ch // 2)]

    def remote(src, dst, sems, k_send, k_recv, seg_to, ch_to):
        return pltpu.make_async_remote_copy(
            src_ref=src,
            dst_ref=dst,
            send_sem=sems[0].at[k_send],
            recv_sem=sems[1].at[k_recv],
            device_id=(seg_to, ch_to),
            device_id_type=MESH,
        )

    sent = []

    def send(*args):
        copy = remote(*args)
        copy.start()
        sent.append(copy)

    load_owners = pltpu.make_async_copy(picks_ref, owners_ref, small_sem.at[0])
    load_owners.start()
    barrier = pltpu.get_barrier_semaphore()
    for place in cross + near[1:]:
        pl.semaphore_signal(barrier, inc=1, device_id=(seg, place), device_id_type=MESH)
    for place in near:
        pl.semaphore_signal(barrier, inc=1, device_id=(other, place), device_id_type=MESH)

    for wide in (wide_here, wide_there):
        wide[n_total:, :] = jnp.zeros((L, steps * c_dev), wide.dtype)
    v_dev = lax.broadcasted_iota(jnp.int32, (s_dev, c_dev), 0).astype(jnp.float32) - mid_dev

    def code(block):
        v = v_dev[:, : block.shape[1]]
        level = jnp.sum(block, axis=0, keepdims=True) / s_dev
        slope = jnp.sum(v * block, axis=0, keepdims=True) / spread_dev
        rest = block - level - slope * v
        top = jnp.maximum(jnp.max(jnp.abs(rest), axis=0, keepdims=True), TINY)
        return level, slope, top / STEPS, jnp.round(rest * (STEPS / top))

    for o in range(n_ch):
        block = strain_ref[:, o * c_dev : (o + 1) * c_dev]
        mine[o] = block
        level, slope, scale, codes = code(block)
        q_out[o] = codes.astype(jnp.int32).astype(jnp.int16)
        st_out[o, 0:3, :] = jnp.concatenate([level, slope, scale], axis=0)

    load_owners.wait()
    blocks = jnp.concatenate(
        [mine[owners_ref[n_panels, p]] for p in range(n_panels)],
        axis=1,
    )
    targets = jnp.concatenate(
        [picks_ref[p : p + 1, :panel_w] + p * c_dev for p in range(n_panels)], axis=1
    )
    hot = (
        lax.broadcasted_iota(jnp.int32, (n_panels * c_dev, width), 0) == targets
    ).astype(jnp.float32)
    picked = jnp.dot(
        blocks, hot, precision=lax.Precision.HIGHEST, preferred_element_type=jnp.float32
    )
    level, slope, scale, codes = code(picked)
    ref_rows = jnp.concatenate(
        [jnp.concatenate([level, slope], axis=1), jnp.concatenate([scale, scale], axis=1)], axis=0
    )
    st_out[:, 3:5, :] = jnp.broadcast_to(ref_rows[None], (n_ch, 2, LANES))
    turned = codes.T
    rq[seg, low, high] = (
        jnp.concatenate([turned[:half], turned[half:]], axis=1)
        .astype(jnp.int32)
        .astype(jnp.int16)
    )
    st_in[seg, me] = st_out[me]

    pl.semaphore_wait(barrier, n_ch - 1 + len(near))

    hops = [(j, x) for j in range(2) for x in range(0, group, 2)]

    def hop_refs(h, k):
        block = rq.at[seg, low, h]
        for place, (j, x) in enumerate(hops[1:]):
            sem = place * n_high + k
            send(block, block, (x_send, x_recv), sem, sem, (seg + j) % 2, partner(x))

    def to_twin(place):
        j, x = hops[place]
        block = rq.at[(seg + j) % 2, partner(x) % group]
        send(block, block, (t_send, t_recv), place, place, seg, partner(1))

    z_ks = range(group, n_ch, group)
    for k in z_ks:
        block = rq.at[seg, low, high]
        send(block, block, (z_send, z_recv), k // group, k // group, seg, partner(k))
    hop_refs(high, 0)
    for place in cross + near[1:]:
        send(st_out.at[place], st_in.at[seg, me], (s_send, s_recv), place, me, seg, place)
    in_q = (q_send.at[0], q_recv.at[0])
    out_q = (q_send.at[1], q_recv.at[1])
    for place, direct in zip(cross, near[n_ch // 4 :] + near[: n_ch // 4]):
        send(q_out.at[place], q_in.at[seg, me], in_q, place, me, seg, place)
        send(q_out.at[direct], q_in.at[seg, me], out_q, direct, me, other, direct)
    for place in near[1:]:
        send(q_out.at[place], q_in.at[seg, me], in_q, place, me, seg, place)

    def lines(which):
        st = st_in[which]
        centre = (
            lax.broadcasted_iota(jnp.int32, (n_ch, 1, LANES), 0) * s_dev
        ).astype(jnp.float32) + (mid_dev - mid_time)
        level = jnp.sum(st[:, 0:1, :], axis=0) / n_ch
        moment = s_dev * centre * st[:, 0:1, :] + spread_dev * st[:, 1:2, :]
        slope = jnp.sum(moment, axis=0) / spread
        return st, centre, level, slope

    def convert(which, level, slope, source, codes):
        wide = wide_here if which is seg else wide_there
        coef = st_in[which, source]
        centre = (source * s_dev).astype(jnp.float32) + (mid_dev - mid_time)
        first = coef[0:1] - level - slope * centre
        second = coef[1:2] - slope
        rest = codes.astype(jnp.int32).astype(jnp.float32) * coef[2:3]
        block = (rest + first + second * v_dev).astype(wide.dtype)
        for a in range(steps):
            row = L + source * s_dev - seg * lag_dev - a * SHIFTS
            rows = pl.ds(pl.multiple_of(row, SHIFTS), s_dev)
            wide[rows, a * c_dev : (a + 1) * c_dev] = block

    def arrive(sems, buf, k):
        remote(buf, buf, sems, k, k, seg, partner(1)).wait_recv()

    is_left = lax.broadcasted_iota(jnp.int32, (half, LANES), 1) < s_dev
    lane = lax.broadcasted_iota(jnp.int32, (1, LANES), 1)
    time_id = lax.broadcasted_iota(jnp.int32, (n_ch, n_total), 1)
    in_part = time_id // s_dev == lax.broadcasted_iota(jnp.int32, (n_ch, n_total), 0)
    ones = in_part.astype(jnp.float32)
    ramps = jnp.where(in_part, (time_id % s_dev).astype(jnp.float32) - mid_dev, 0.0)
    patterns = jnp.concatenate([ones, ramps], axis=0)

    def expand(s, plane):
        st = [st_in[s, i] for i in range(n_ch)]
        centres = [i * s_dev + mid_dev - mid_time for i in range(n_ch)]
        both = sum(st[i][3:4] for i in range(n_ch))
        moved = sum(centres[i] * st[i][3:4] for i in range(n_ch))
        ref_stat = jnp.where(
            lane < width,
            both / n_ch,
            (s_dev * pltpu.roll(moved, width, 1) + spread_dev * both) / spread,
        )
        ref_slope = pltpu.roll(ref_stat, width, 1)
        first = jnp.concatenate(
            [
                st[i][3:4] - jnp.where(lane < width, ref_stat + centres[i] * ref_slope, ref_stat)
                for i in range(n_ch)
            ],
            axis=0,
        )
        scale = jnp.concatenate([st[i][4:5] for i in range(n_ch)], axis=0)
        coefs = jnp.concatenate([first, pltpu.roll(first, width, 1)], axis=0)

        def along(rows, pattern):
            return lax.dot_general(
                rows,
                pattern,
                (((0,), (0,)), ((), ())),
                precision=lax.Precision.HIGHEST,
                preferred_element_type=jnp.float32,
            )[:width]

        maps[plane, 0] = along(scale, ones)
        maps[plane, 1] = along(coefs, patterns)

    def ref_series(s, plane):
        tops, lows = [], []
        for i in range(0, n_ch, 2):
            one = rq[s, i % group, i // group].astype(jnp.int32).astype(jnp.float32)
            two = rq[s, (i + 1) % group, (i + 1) // group].astype(jnp.int32).astype(jnp.float32)
            tops.append(jnp.where(is_left, one, pltpu.roll(two, s_dev, 1)))
            lows.append(jnp.where(is_left, pltpu.roll(one, s_dev, 1), two))
        series = jnp.concatenate(
            [jnp.concatenate(tops, axis=1), jnp.concatenate(lows, axis=1)], axis=0
        )
        return (series * maps[plane, 0] + maps[plane, 1]).astype(rt_here.dtype)

    def shift_refs(series, rt, b):
        moved = series
        if b:
            blank = jnp.zeros((width, b), rt.dtype)
            moved = jnp.concatenate([blank, series[:, : n_total - b]], axis=1)
        rt[b * width : (b + 1) * width, :] = moved

    def hop_far_refs():
        for k in z_ks:
            h = partner(k) // group
            arrive((z_send, z_recv), rq.at[seg, low, h], k // group)
            hop_refs(h, k // group)
        to_twin(0)

    def take_lines():
        for place in cross + near[1:]:
            arrive((s_send, s_recv), st_in.at[seg, place], place)
        send(st_in.at[seg], st_in.at[seg], (y_send, y_recv), 0, 0, other, me)
        return lines(seg)[2:]

    def hand_over(places):
        for place in places:
            block = q_in.at[seg, place]
            arrive(in_q, block, place)
            send(block, block, out_q, place, place, other, me)

    def pass_to_twin():
        for hop in range(1, len(hops)):
            j, x = hops[hop]
            for h in range(n_high):
                row = partner(h * group) // group
                block = rq.at[(seg + j) % 2, partner(x) % group, row]
                arrive((x_send, x_recv), block, (hop - 1) * n_high + h)
            to_twin(hop)

    def convert_here(places):
        for place in places:
            convert(seg, level, slope, place, q_in[seg, place])

    hop_far_refs()
    level, slope = take_lines()
    expand(seg, 0)
    convert(seg, level, slope, me, q_out[me])
    hand_over(cross[0:1])
    convert_here(cross[0:1])
    hand_over(cross[1:2])
    convert_here(cross[1:2])
    hand_over(cross[2:3])
    convert_here(cross[2:3])
    hand_over(cross[3:4])
    convert_here(cross[3:4])
    hand_over(cross[4:5])
    convert_here(cross[4:5])
    hand_over(cross[5:6])
    convert_here(cross[5:6])
    pass_to_twin()
    hand_over(cross[6:7])
    convert_here(cross[6:7])
    hand_over(cross[7:8])
    convert_here(cross[7:8])
    for place in near[1:]:
        arrive(in_q, q_in.at[seg, place], place)
        convert(seg, level, slope, place, q_in[seg, place])
    arrive((y_send, y_recv), st_in.at[other], 0)
    _, _, other_level, other_slope = lines(other)
    expand(other, 1)
    for place in near:
        block = q_in.at[other, place]
        arrive(out_q, block, place)
        convert(other, other_level, other_slope, place, q_in[other, place])
    for place, (j, x) in enumerate(hops):
        arrive((t_send, t_recv), rq.at[(seg + j) % 2, partner(x + 1) % group], place)

    quad = 4
    rows = quad * width

    def product(rt, wide, j):
        return jnp.dot(
            rt[j * rows : (j + 1) * rows, :],
            wide[L : L + n_total, :],
            preferred_element_type=jnp.float32,
        )

    series = ref_series(seg, 0)
    for b in range(SHIFTS):
        shift_refs(series, rt_here, b)
    series = ref_series(other, 1)
    for j in range(SHIFTS // quad):
        acc[j] = product(rt_here, wide_here, j)
        for b in range(j * quad, (j + 1) * quad):
            shift_refs(series, rt_there, b)
    for place in cross:
        block = q_in.at[other, place]
        arrive(out_q, block, place)
        convert(other, other_level, other_slope, place, q_in[other, place])
    base = (seg * lag_dev).astype(jnp.float32)
    for j in range(SHIFTS // quad):
        total = acc[j] + product(rt_there, wide_there, j)
        for a in range(steps):
            for b in range(quad):
                k = a * SHIFTS + j * quad + b
                block = total[b * width : (b + 1) * width, a * c_dev : (a + 1) * c_dev]
                out_ref[k] = block * (1.0 / (2 * (n_total - (base + k))))
    for copy in sent:
        copy.wait_send()


def wide_blocks(strain, ref_local, owners):
    my_rows = strain[0]
    s_dev, chans = my_rows.shape
    n_ch = lax.axis_size("ch")
    n_seg = lax.axis_size("seg")
    n_total = s_dev * n_ch
    c_dev = chans // n_ch
    group = max(g for g in range(1, math.isqrt(n_ch) + 1) if n_ch % g == 0)
    n_high = n_ch // group
    width = ref_local.shape[0] * ref_local.shape[1]
    lag_dev = L // n_seg
    steps = lag_dev // SHIFTS
    line = jnp.pad(owners, (0, ref_local.shape[1] - owners.shape[0]))
    picks = jnp.concatenate([ref_local, line[None]], axis=0)
    vmem = pl.BlockSpec(memory_space=pltpu.VMEM)
    dma = pltpu.SemaphoreType.DMA
    turned = pl.pallas_call(
        functools.partial(fused_kernel, n_ch, group, width),
        out_shape=jax.ShapeDtypeStruct((lag_dev, width, c_dev), jnp.float32),
        in_specs=[vmem, vmem],
        out_specs=vmem,
        scratch_shapes=[
            pltpu.SMEM(picks.shape, jnp.int32),
            pltpu.VMEM((n_ch, s_dev, c_dev), jnp.float32),
            pltpu.VMEM((n_ch, s_dev, c_dev), jnp.int16),
            pltpu.VMEM((n_ch, 5, c_dev), jnp.float32),
            pltpu.VMEM((n_seg, n_ch, s_dev, c_dev), jnp.int16),
            pltpu.VMEM((n_seg, n_ch, 5, c_dev), jnp.float32),
            pltpu.VMEM((n_seg, group, n_high, width // 2, LANES), jnp.int16),
            pltpu.VMEM((L + n_total, steps * c_dev), jnp.bfloat16),
            pltpu.VMEM((L + n_total, steps * c_dev), jnp.bfloat16),
            pltpu.VMEM((SHIFTS * width, n_total), jnp.bfloat16),
            pltpu.VMEM((SHIFTS * width, n_total), jnp.bfloat16),
            pltpu.VMEM((n_seg, 2, width, n_total), jnp.float32),
            pltpu.VMEM((SHIFTS // 4, 4 * width, steps * c_dev), jnp.float32),
            dma((1,)),
            dma((n_ch,)), dma((n_ch,)),
            dma((n_seg, n_ch)), dma((n_seg, n_ch)),
            dma((n_high,)), dma((n_high,)),
            dma((n_seg * group * n_high,)), dma((n_seg * group * n_high,)),
            dma((n_seg * group,)), dma((n_seg * group,)),
            dma((1,)), dma((1,)),
        ],
        compiler_params=pltpu.CompilerParams(
            collective_id=0, has_side_effects=True, vmem_limit_bytes=GRANT
        ),
    )(my_rows, picks)
    return turned.transpose(0, 2, 1)


def solution(mesh):
    n_seg, n_ch = mesh.shape["seg"], mesh.shape["ch"]

    def per_device(strain, ref_local, owners):
        s_dev, chans = strain.shape[1:]
        fits = (
            chans == n_ch * LANES
            and n_seg == 2
            and (L // n_seg) % SHIFTS == 0
            and 2 * s_dev == LANES
            and n_ch >= 4
            and n_ch & (n_ch - 1) == 0
            and 2 * ref_local.size == LANES
            and ref_local.shape[0] <= ref_local.shape[1]
        )
        return (wide_blocks if fits else narrow_blocks)(strain, ref_local, owners)

    in_specs = (P("seg", "ch", None), P(), P())
    out_specs = P("seg", "ch", None)
    return jax.shard_map(
        per_device, mesh=mesh, in_specs=in_specs, out_specs=out_specs, check_vma=False
    )
```

```python
import functools
import math

import jax
import jax.numpy as jnp
from jax import lax
from jax.experimental import pallas as pl
from jax.experimental.pallas import tpu as pltpu
from jax.sharding import PartitionSpec as P

L = 64
LANES = 128
SHIFTS = 16
GRANT = 24 * 1024 * 1024
STEPS = 32000.0
TINY = 1e-33
MESH = pl.DeviceIdType.MESH


def spread_2(block, axis, holder):
    block = jnp.where(lax.axis_index(axis) == holder, block, jnp.zeros_like(block))
    return lax.psum(block, axis)


def detrend_cols(series):
    n_total = series.shape[0]
    mid_time = (n_total - 1) / 2.0
    spread = n_total * (n_total * n_total - 1) / 12.0
    centred = (jnp.arange(n_total, dtype=jnp.float32) - mid_time)[:, None]
    level_val = jnp.sum(series, axis=0) / n_total
    slope_val = jnp.sum(centred * series, axis=0) / spread
    return (series - level_val - slope_val * centred).astype(jnp.bfloat16)


def owner_panels(detrended, ref_local, owners):
    pieces = []
    for panel_id in range(ref_local.shape[0]):
        own_cols = jnp.take(detrended, ref_local[panel_id], axis=1)
        pieces.append(spread_2(own_cols, "ch", owners[panel_id]))
    return jnp.concatenate(pieces, axis=1)


def narrow_blocks(strain, ref_local, owners):
    my_rows = strain[0]
    s_dev, chans = my_rows.shape
    n_ch = lax.axis_size("ch")
    n_seg = lax.axis_size("seg")
    n_total = s_dev * n_ch
    c_dev = chans // n_ch
    series = lax.all_to_all(my_rows, "ch", split_axis=1, concat_axis=0, tiled=True)
    detrended = detrend_cols(series)
    panels = owner_panels(detrended, ref_local, owners)
    width_ref = panels.shape[1]
    padded = jnp.concatenate([detrended, jnp.zeros((L, c_dev), jnp.bfloat16)], axis=0)
    blk_rows = min(512, n_total)
    n_blocks = n_total // blk_rows
    lag_dev = L // n_seg
    lag_count = lax.axis_size("seg") * lag_dev

    def add_block(blk_idx, running):
        blk_start = blk_idx * blk_rows
        window = lax.dynamic_slice_in_dim(padded, blk_start, blk_rows + lag_count - 1, 0)
        lagged = jnp.concatenate(
            [window[lag_off : lag_off + blk_rows] for lag_off in range(lag_count)], axis=1
        )
        ref_block = lax.dynamic_slice_in_dim(panels, blk_start, blk_rows, 0)
        return running + lax.dot_general(
            lagged, ref_block, (((0,), (0,)), ((), ())), preferred_element_type=jnp.float32
        )

    start_acc = jnp.zeros((lag_count * c_dev, width_ref), jnp.float32)
    running = lax.fori_loop(0, n_blocks, add_block, start_acc)
    summed = lax.psum_scatter(
        running.reshape(lag_count, c_dev, width_ref), "seg", scatter_dimension=0, tiled=True
    )
    lag_ids = (lax.axis_index("seg") * lag_dev + jnp.arange(lag_dev, dtype=jnp.int32)).astype(
        jnp.float32
    )
    return summed / (n_seg * (n_total - lag_ids))[:, None, None]


def fused_kernel(
    n_ch, group, width, strain_ref, picks_ref, out_ref,
    owners_ref, mine, q_out, st_out, q_in, st_in, rq, wide_here, wide_there, rt_here, rt_there, maps, acc,
    small_sem, s_send, s_recv, q_send, q_recv, z_send, z_recv,
    x_send, x_recv, t_send, t_recv, y_send, y_recv,
):
    seg = lax.axis_index("seg")
    me = lax.axis_index("ch")
    other = 1 - seg
    high, low = me // group, me % group
    n_high = n_ch // group
    s_dev = strain_ref.shape[0]
    c_dev = strain_ref.shape[1] // n_ch
    n_total = s_dev * n_ch
    n_panels = picks_ref.shape[0] - 1
    panel_w = width // n_panels
    lag_dev = out_ref.shape[0]
    steps = lag_dev // SHIFTS
    mid_time = (n_total - 1) / 2.0
    spread = n_total * (n_total * n_total - 1) / 12.0
    mid_dev = (s_dev - 1) / 2.0
    spread_dev = s_dev * (s_dev * s_dev - 1) / 12.0
    half = width // 2
    upper = me // (n_ch // 2)

    def flip(place, k):
        bit = 1
        while bit <= k:
            if k & bit:
                place = place + (1 - 2 * ((me // bit) % 2)) * bit
            bit *= 2
        return place

    def partner(k):
        return flip(me, k)

    def far(p):
        row = (1 - upper) * (n_high // 2) + p // group
        place = p % group
        return row * group + place // 2 * 2 + (me + place) % 2

    near = [partner(k) for k in range(n_ch // 2)]
    cross = [far(p) for p in range(n_ch // 2)]

    def remote(src, dst, sems, k_send, k_recv, seg_to, ch_to):
        return pltpu.make_async_remote_copy(
            src_ref=src,
            dst_ref=dst,
            send_sem=sems[0].at[k_send],
            recv_sem=sems[1].at[k_recv],
            device_id=(seg_to, ch_to),
            device_id_type=MESH,
        )

    sent = []

    def send(*args):
        copy = remote(*args)
        copy.start()
        sent.append(copy)

    load_owners = pltpu.make_async_copy(picks_ref, owners_ref, small_sem.at[0])
    load_owners.start()
    barrier = pltpu.get_barrier_semaphore()
    for place in cross + near[1:]:
        pl.semaphore_signal(barrier, inc=1, device_id=(seg, place), device_id_type=MESH)
    for place in near:
        pl.semaphore_signal(barrier, inc=1, device_id=(other, place), device_id_type=MESH)

    for wide in (wide_here, wide_there):
        wide[n_total:, :] = jnp.zeros((L, steps * c_dev), wide.dtype)
    v_dev = lax.broadcasted_iota(jnp.int32, (s_dev, c_dev), 0).astype(jnp.float32) - mid_dev

    def code(block):
        v = v_dev[:, : block.shape[1]]
        level = jnp.sum(block, axis=0, keepdims=True) / s_dev
        slope = jnp.sum(v * block, axis=0, keepdims=True) / spread_dev
        rest = block - level - slope * v
        top = jnp.maximum(jnp.max(jnp.abs(rest), axis=0, keepdims=True), TINY)
        return level, slope, top / STEPS, jnp.round(rest * (STEPS / top))

    for o in range(n_ch):
        block = strain_ref[:, o * c_dev : (o + 1) * c_dev]
        mine[o] = block
        level, slope, scale, codes = code(block)
        q_out[o] = codes.astype(jnp.int32).astype(jnp.int16)
        st_out[o, 0:3, :] = jnp.concatenate([level, slope, scale], axis=0)

    load_owners.wait()
    blocks = jnp.concatenate(
        [mine[owners_ref[n_panels, p]] for p in range(n_panels)],
        axis=1,
    )
    targets = jnp.concatenate(
        [picks_ref[p : p + 1, :panel_w] + p * c_dev for p in range(n_panels)], axis=1
    )
    hot = (
        lax.broadcasted_iota(jnp.int32, (n_panels * c_dev, width), 0) == targets
    ).astype(jnp.float32)
    picked = jnp.dot(
        blocks, hot, precision=lax.Precision.HIGHEST, preferred_element_type=jnp.float32
    )
    level, slope, scale, codes = code(picked)
    ref_rows = jnp.concatenate(
        [jnp.concatenate([level, slope], axis=1), jnp.concatenate([scale, scale], axis=1)], axis=0
    )
    st_out[:, 3:5, :] = jnp.broadcast_to(ref_rows[None], (n_ch, 2, LANES))
    turned = codes.T
    rq[seg, low, high] = (
        jnp.concatenate([turned[:half], turned[half:]], axis=1)
        .astype(jnp.int32)
        .astype(jnp.int16)
    )
    st_in[seg, me] = st_out[me]

    pl.semaphore_wait(barrier, n_ch - 1 + len(near))

    hops = [(j, x) for j in range(2) for x in range(0, group, 2)]

    def hop_refs(h, k):
        block = rq.at[seg, low, h]
        for place, (j, x) in enumerate(hops[1:]):
            sem = place * n_high + k
            send(block, block, (x_send, x_recv), sem, sem, (seg + j) % 2, partner(x))

    def to_twin(place):
        j, x = hops[place]
        block = rq.at[(seg + j) % 2, partner(x) % group]
        send(block, block, (t_send, t_recv), place, place, seg, partner(1))

    z_ks = range(group, n_ch, group)
    for k in z_ks:
        block = rq.at[seg, low, high]
        send(block, block, (z_send, z_recv), k // group, k // group, seg, partner(k))
    for place in cross + near[1:]:
        send(st_out.at[place], st_in.at[seg, me], (s_send, s_recv), place, me, seg, place)
    hop_refs(high, 0)
    in_q = (q_send.at[0], q_recv.at[0])
    out_q = (q_send.at[1], q_recv.at[1])
    for place, direct in zip(cross, near[n_ch // 4 :] + near[: n_ch // 4]):
        send(q_out.at[place], q_in.at[seg, me], in_q, place, me, seg, place)
        send(q_out.at[direct], q_in.at[seg, me], out_q, direct, me, other, direct)
    for place in near[1:]:
        send(q_out.at[place], q_in.at[seg, me], in_q, place, me, seg, place)

    def lines(which):
        st = st_in[which]
        centre = (
            lax.broadcasted_iota(jnp.int32, (n_ch, 1, LANES), 0) * s_dev
        ).astype(jnp.float32) + (mid_dev - mid_time)
        level = jnp.sum(st[:, 0:1, :], axis=0) / n_ch
        moment = s_dev * centre * st[:, 0:1, :] + spread_dev * st[:, 1:2, :]
        slope = jnp.sum(moment, axis=0) / spread
        return st, centre, level, slope

    def convert(which, level, slope, source, codes):
        wide = wide_here if which is seg else wide_there
        coef = st_in[which, source]
        centre = (source * s_dev).astype(jnp.float32) + (mid_dev - mid_time)
        first = coef[0:1] - level - slope * centre
        second = coef[1:2] - slope
        rest = codes.astype(jnp.int32).astype(jnp.float32) * coef[2:3]
        block = (rest + first + second * v_dev).astype(wide.dtype)
        for a in range(steps):
            row = L + source * s_dev - seg * lag_dev - a * SHIFTS
            rows = pl.ds(pl.multiple_of(row, SHIFTS), s_dev)
            wide[rows, a * c_dev : (a + 1) * c_dev] = block

    def arrive(sems, buf, k):
        remote(buf, buf, sems, k, k, seg, partner(1)).wait_recv()

    is_left = lax.broadcasted_iota(jnp.int32, (half, LANES), 1) < s_dev
    lane = lax.broadcasted_iota(jnp.int32, (1, LANES), 1)
    time_id = lax.broadcasted_iota(jnp.int32, (n_ch, n_total), 1)
    in_part = time_id // s_dev == lax.broadcasted_iota(jnp.int32, (n_ch, n_total), 0)
    ones = in_part.astype(jnp.float32)
    ramps = jnp.where(in_part, (time_id % s_dev).astype(jnp.float32) - mid_dev, 0.0)
    patterns = jnp.concatenate([ones, ramps], axis=0)

    def expand(s, plane):
        st = [st_in[s, i] for i in range(n_ch)]
        centres = [i * s_dev + mid_dev - mid_time for i in range(n_ch)]
        both = sum(st[i][3:4] for i in range(n_ch))
        moved = sum(centres[i] * st[i][3:4] for i in range(n_ch))
        ref_stat = jnp.where(
            lane < width,
            both / n_ch,
            (s_dev * pltpu.roll(moved, width, 1) + spread_dev * both) / spread,
        )
        ref_slope = pltpu.roll(ref_stat, width, 1)
        first = jnp.concatenate(
            [
                st[i][3:4] - jnp.where(lane < width, ref_stat + centres[i] * ref_slope, ref_stat)
                for i in range(n_ch)
            ],
            axis=0,
        )
        scale = jnp.concatenate([st[i][4:5] for i in range(n_ch)], axis=0)
        coefs = jnp.concatenate([first, pltpu.roll(first, width, 1)], axis=0)

        def along(rows, pattern):
            return lax.dot_general(
                rows,
                pattern,
                (((0,), (0,)), ((), ())),
                precision=lax.Precision.HIGHEST,
                preferred_element_type=jnp.float32,
            )[:width]

        maps[plane, 0] = along(scale, ones)
        maps[plane, 1] = along(coefs, patterns)

    def ref_series(s, plane):
        tops, lows = [], []
        for i in range(0, n_ch, 2):
            one = rq[s, i % group, i // group].astype(jnp.int32).astype(jnp.float32)
            two = rq[s, (i + 1) % group, (i + 1) // group].astype(jnp.int32).astype(jnp.float32)
            tops.append(jnp.where(is_left, one, pltpu.roll(two, s_dev, 1)))
            lows.append(jnp.where(is_left, pltpu.roll(one, s_dev, 1), two))
        series = jnp.concatenate(
            [jnp.concatenate(tops, axis=1), jnp.concatenate(lows, axis=1)], axis=0
        )
        return (series * maps[plane, 0] + maps[plane, 1]).astype(rt_here.dtype)

    def shift_refs(series, rt, b):
        moved = series
        if b:
            blank = jnp.zeros((width, b), rt.dtype)
            moved = jnp.concatenate([blank, series[:, : n_total - b]], axis=1)
        rt[b * width : (b + 1) * width, :] = moved

    def hop_far_refs():
        for k in z_ks:
            h = partner(k) // group
            arrive((z_send, z_recv), rq.at[seg, low, h], k // group)
            hop_refs(h, k // group)
        to_twin(0)

    def take_lines():
        for place in cross + near[1:]:
            arrive((s_send, s_recv), st_in.at[seg, place], place)
        send(st_in.at[seg], st_in.at[seg], (y_send, y_recv), 0, 0, other, me)
        return lines(seg)[2:]

    def hand_over(places):
        for place in places:
            block = q_in.at[seg, place]
            arrive(in_q, block, place)
            send(block, block, out_q, place, place, other, me)

    def pass_to_twin():
        for hop in range(1, len(hops)):
            j, x = hops[hop]
            for h in range(n_high):
                row = partner(h * group) // group
                block = rq.at[(seg + j) % 2, partner(x) % group, row]
                arrive((x_send, x_recv), block, (hop - 1) * n_high + h)
            to_twin(hop)

    def convert_here(places):
        for place in places:
            convert(seg, level, slope, place, q_in[seg, place])

    hop_far_refs()
    level, slope = take_lines()
    expand(seg, 0)
    convert(seg, level, slope, me, q_out[me])
    hand_over(cross[0:1])
    convert_here(cross[0:1])
    hand_over(cross[1:2])
    convert_here(cross[1:2])
    hand_over(cross[2:3])
    convert_here(cross[2:3])
    hand_over(cross[3:4])
    convert_here(cross[3:4])
    hand_over(cross[4:5])
    convert_here(cross[4:5])
    hand_over(cross[5:6])
    convert_here(cross[5:6])
    pass_to_twin()
    hand_over(cross[6:7])
    convert_here(cross[6:7])
    hand_over(cross[7:8])
    convert_here(cross[7:8])
    for place in near[1:]:
        arrive(in_q, q_in.at[seg, place], place)
        convert(seg, level, slope, place, q_in[seg, place])
    arrive((y_send, y_recv), st_in.at[other], 0)
    _, _, other_level, other_slope = lines(other)
    expand(other, 1)
    for place in near:
        block = q_in.at[other, place]
        arrive(out_q, block, place)
        convert(other, other_level, other_slope, place, q_in[other, place])
    for place, (j, x) in enumerate(hops):
        arrive((t_send, t_recv), rq.at[(seg + j) % 2, partner(x + 1) % group], place)

    quad = 4
    rows = quad * width

    def product(rt, wide, j):
        return jnp.dot(
            rt[j * rows : (j + 1) * rows, :],
            wide[L : L + n_total, :],
            preferred_element_type=jnp.float32,
        )

    series = ref_series(seg, 0)
    for b in range(SHIFTS):
        shift_refs(series, rt_here, b)
    series = ref_series(other, 1)
    for j in range(SHIFTS // quad):
        acc[j] = product(rt_here, wide_here, j)
        for b in range(j * quad, (j + 1) * quad):
            shift_refs(series, rt_there, b)
    for place in cross:
        block = q_in.at[other, place]
        arrive(out_q, block, place)
        convert(other, other_level, other_slope, place, q_in[other, place])
    base = (seg * lag_dev).astype(jnp.float32)
    for j in range(SHIFTS // quad):
        total = acc[j] + product(rt_there, wide_there, j)
        for a in range(steps):
            for b in range(quad):
                k = a * SHIFTS + j * quad + b
                block = total[b * width : (b + 1) * width, a * c_dev : (a + 1) * c_dev]
                out_ref[k] = block * (1.0 / (2 * (n_total - (base + k))))
    for copy in sent:
        copy.wait_send()


def wide_blocks(strain, ref_local, owners):
    my_rows = strain[0]
    s_dev, chans = my_rows.shape
    n_ch = lax.axis_size("ch")
    n_seg = lax.axis_size("seg")
    n_total = s_dev * n_ch
    c_dev = chans // n_ch
    group = max(g for g in range(1, math.isqrt(n_ch) + 1) if n_ch % g == 0)
    n_high = n_ch // group
    width = ref_local.shape[0] * ref_local.shape[1]
    lag_dev = L // n_seg
    steps = lag_dev // SHIFTS
    line = jnp.pad(owners, (0, ref_local.shape[1] - owners.shape[0]))
    picks = jnp.concatenate([ref_local, line[None]], axis=0)
    vmem = pl.BlockSpec(memory_space=pltpu.VMEM)
    dma = pltpu.SemaphoreType.DMA
    turned = pl.pallas_call(
        functools.partial(fused_kernel, n_ch, group, width),
        out_shape=jax.ShapeDtypeStruct((lag_dev, width, c_dev), jnp.float32),
        in_specs=[vmem, vmem],
        out_specs=vmem,
        scratch_shapes=[
            pltpu.SMEM(picks.shape, jnp.int32),
            pltpu.VMEM((n_ch, s_dev, c_dev), jnp.float32),
            pltpu.VMEM((n_ch, s_dev, c_dev), jnp.int16),
            pltpu.VMEM((n_ch, 5, c_dev), jnp.float32),
            pltpu.VMEM((n_seg, n_ch, s_dev, c_dev), jnp.int16),
            pltpu.VMEM((n_seg, n_ch, 5, c_dev), jnp.float32),
            pltpu.VMEM((n_seg, group, n_high, width // 2, LANES), jnp.int16),
            pltpu.VMEM((L + n_total, steps * c_dev), jnp.bfloat16),
            pltpu.VMEM((L + n_total, steps * c_dev), jnp.bfloat16),
            pltpu.VMEM((SHIFTS * width, n_total), jnp.bfloat16),
            pltpu.VMEM((SHIFTS * width, n_total), jnp.bfloat16),
            pltpu.VMEM((n_seg, 2, width, n_total), jnp.float32),
            pltpu.VMEM((SHIFTS // 4, 4 * width, steps * c_dev), jnp.float32),
            dma((1,)),
            dma((n_ch,)), dma((n_ch,)),
            dma((n_seg, n_ch)), dma((n_seg, n_ch)),
            dma((n_high,)), dma((n_high,)),
            dma((n_seg * group * n_high,)), dma((n_seg * group * n_high,)),
            dma((n_seg * group,)), dma((n_seg * group,)),
            dma((1,)), dma((1,)),
        ],
        compiler_params=pltpu.CompilerParams(
            collective_id=0, has_side_effects=True, vmem_limit_bytes=GRANT
        ),
    )(my_rows, picks)
    return turned.transpose(0, 2, 1)


def solution(mesh):
    n_seg, n_ch = mesh.shape["seg"], mesh.shape["ch"]

    def per_device(strain, ref_local, owners):
        s_dev, chans = strain.shape[1:]
        fits = (
            chans == n_ch * LANES
            and n_seg == 2
            and (L // n_seg) % SHIFTS == 0
            and 2 * s_dev == LANES
            and n_ch >= 4
            and n_ch & (n_ch - 1) == 0
            and 2 * ref_local.size == LANES
            and ref_local.shape[0] <= ref_local.shape[1]
        )
        return (wide_blocks if fits else narrow_blocks)(strain, ref_local, owners)

    in_specs = (P("seg", "ch", None), P(), P())
    out_specs = P("seg", "ch", None)
    return jax.shard_map(
        per_device, mesh=mesh, in_specs=in_specs, out_specs=out_specs, check_vma=False
    )
```

```python
import functools
import math

import jax
import jax.numpy as jnp
from jax import lax
from jax.experimental import pallas as pl
from jax.experimental.pallas import tpu as pltpu
from jax.sharding import PartitionSpec as P

L = 64
LANES = 128
SHIFTS = 16
GRANT = 24 * 1024 * 1024
STEPS = 32000.0
TINY = 1e-33
MESH = pl.DeviceIdType.MESH


def spread_2(block, axis, holder):
    block = jnp.where(lax.axis_index(axis) == holder, block, jnp.zeros_like(block))
    return lax.psum(block, axis)


def detrend_cols(series):
    n_total = series.shape[0]
    mid_time = (n_total - 1) / 2.0
    spread = n_total * (n_total * n_total - 1) / 12.0
    centred = (jnp.arange(n_total, dtype=jnp.float32) - mid_time)[:, None]
    level_val = jnp.sum(series, axis=0) / n_total
    slope_val = jnp.sum(centred * series, axis=0) / spread
    return (series - level_val - slope_val * centred).astype(jnp.bfloat16)


def owner_panels(detrended, ref_local, owners):
    pieces = []
    for panel_id in range(ref_local.shape[0]):
        own_cols = jnp.take(detrended, ref_local[panel_id], axis=1)
        pieces.append(spread_2(own_cols, "ch", owners[panel_id]))
    return jnp.concatenate(pieces, axis=1)


def narrow_blocks(strain, ref_local, owners):
    my_rows = strain[0]
    s_dev, chans = my_rows.shape
    n_ch = lax.axis_size("ch")
    n_seg = lax.axis_size("seg")
    n_total = s_dev * n_ch
    c_dev = chans // n_ch
    series = lax.all_to_all(my_rows, "ch", split_axis=1, concat_axis=0, tiled=True)
    detrended = detrend_cols(series)
    panels = owner_panels(detrended, ref_local, owners)
    width_ref = panels.shape[1]
    padded = jnp.concatenate([detrended, jnp.zeros((L, c_dev), jnp.bfloat16)], axis=0)
    blk_rows = min(512, n_total)
    n_blocks = n_total // blk_rows
    lag_dev = L // n_seg
    lag_count = lax.axis_size("seg") * lag_dev

    def add_block(blk_idx, running):
        blk_start = blk_idx * blk_rows
        window = lax.dynamic_slice_in_dim(padded, blk_start, blk_rows + lag_count - 1, 0)
        lagged = jnp.concatenate(
            [window[lag_off : lag_off + blk_rows] for lag_off in range(lag_count)], axis=1
        )
        ref_block = lax.dynamic_slice_in_dim(panels, blk_start, blk_rows, 0)
        return running + lax.dot_general(
            lagged, ref_block, (((0,), (0,)), ((), ())), preferred_element_type=jnp.float32
        )

    start_acc = jnp.zeros((lag_count * c_dev, width_ref), jnp.float32)
    running = lax.fori_loop(0, n_blocks, add_block, start_acc)
    summed = lax.psum_scatter(
        running.reshape(lag_count, c_dev, width_ref), "seg", scatter_dimension=0, tiled=True
    )
    lag_ids = (lax.axis_index("seg") * lag_dev + jnp.arange(lag_dev, dtype=jnp.int32)).astype(
        jnp.float32
    )
    return summed / (n_seg * (n_total - lag_ids))[:, None, None]


def fused_kernel(
    n_ch, group, width, strain_ref, picks_ref, out_ref,
    owners_ref, mine, q_out, st_out, q_in, st_in, rq, wide_here, wide_there, rt_here, rt_there, maps, acc,
    small_sem, s_send, s_recv, q_send, q_recv, z_send, z_recv,
    x_send, x_recv, t_send, t_recv, y_send, y_recv,
):
    seg = lax.axis_index("seg")
    me = lax.axis_index("ch")
    other = 1 - seg
    high, low = me // group, me % group
    n_high = n_ch // group
    s_dev = strain_ref.shape[0]
    c_dev = strain_ref.shape[1] // n_ch
    n_total = s_dev * n_ch
    n_panels = picks_ref.shape[0] - 1
    panel_w = width // n_panels
    lag_dev = out_ref.shape[0]
    steps = lag_dev // SHIFTS
    mid_time = (n_total - 1) / 2.0
    spread = n_total * (n_total * n_total - 1) / 12.0
    mid_dev = (s_dev - 1) / 2.0
    spread_dev = s_dev * (s_dev * s_dev - 1) / 12.0
    half = width // 2
    upper = me // (n_ch // 2)

    def flip(place, k):
        bit = 1
        while bit <= k:
            if k & bit:
                place = place + (1 - 2 * ((me // bit) % 2)) * bit
            bit *= 2
        return place

    def partner(k):
        return flip(me, k)

    def far(p):
        row = (1 - upper) * (n_high // 2) + p // group
        place = p % group
        return row * group + place // 2 * 2 + (me + place) % 2

    near = [partner(k) for k in range(n_ch // 2)]
    cross = [far(p) for p in range(n_ch // 2)]

    def remote(src, dst, sems, k_send, k_recv, seg_to, ch_to):
        return pltpu.make_async_remote_copy(
            src_ref=src,
            dst_ref=dst,
            send_sem=sems[0].at[k_send],
            recv_sem=sems[1].at[k_recv],
            device_id=(seg_to, ch_to),
            device_id_type=MESH,
        )

    sent = []

    def send(*args):
        copy = remote(*args)
        copy.start()
        sent.append(copy)

    load_owners = pltpu.make_async_copy(picks_ref, owners_ref, small_sem.at[0])
    load_owners.start()
    barrier = pltpu.get_barrier_semaphore()
    for place in cross + near[1:]:
        pl.semaphore_signal(barrier, inc=1, device_id=(seg, place), device_id_type=MESH)
    for place in near:
        pl.semaphore_signal(barrier, inc=1, device_id=(other, place), device_id_type=MESH)

    for wide in (wide_here, wide_there):
        wide[n_total:, :] = jnp.zeros((L, steps * c_dev), wide.dtype)
    v_dev = lax.broadcasted_iota(jnp.int32, (s_dev, c_dev), 0).astype(jnp.float32) - mid_dev

    def code(block):
        v = v_dev[:, : block.shape[1]]
        level = jnp.sum(block, axis=0, keepdims=True) / s_dev
        slope = jnp.sum(v * block, axis=0, keepdims=True) / spread_dev
        rest = block - level - slope * v
        top = jnp.maximum(jnp.max(jnp.abs(rest), axis=0, keepdims=True), TINY)
        return level, slope, top / STEPS, jnp.round(rest * (STEPS / top))

    for o in range(n_ch):
        block = strain_ref[:, o * c_dev : (o + 1) * c_dev]
        mine[o] = block
        level, slope, scale, codes = code(block)
        q_out[o] = codes.astype(jnp.int32).astype(jnp.int16)
        st_out[o, 0:3, :] = jnp.concatenate([level, slope, scale], axis=0)

    load_owners.wait()
    blocks = jnp.concatenate(
        [mine[owners_ref[n_panels, p]] for p in range(n_panels)],
        axis=1,
    )
    targets = jnp.concatenate(
        [picks_ref[p : p + 1, :panel_w] + p * c_dev for p in range(n_panels)], axis=1
    )
    hot = (
        lax.broadcasted_iota(jnp.int32, (n_panels * c_dev, width), 0) == targets
    ).astype(jnp.float32)
    picked = jnp.dot(
        blocks, hot, precision=lax.Precision.HIGHEST, preferred_element_type=jnp.float32
    )
    level, slope, scale, codes = code(picked)
    ref_rows = jnp.concatenate(
        [jnp.concatenate([level, slope], axis=1), jnp.concatenate([scale, scale], axis=1)], axis=0
    )
    st_out[:, 3:5, :] = jnp.broadcast_to(ref_rows[None], (n_ch, 2, LANES))
    turned = codes.T
    rq[seg, low, high] = (
        jnp.concatenate([turned[:half], turned[half:]], axis=1)
        .astype(jnp.int32)
        .astype(jnp.int16)
    )
    st_in[seg, me] = st_out[me]

    pl.semaphore_wait(barrier, n_ch - 1 + len(near))

    hops = [(j, x) for j in range(2) for x in range(0, group, 2)]

    def hop_refs(h, k):
        block = rq.at[seg, low, h]
        for place, (j, x) in enumerate(hops[1:]):
            sem = place * n_high + k
            send(block, block, (x_send, x_recv), sem, sem, (seg + j) % 2, partner(x))

    def to_twin(place):
        j, x = hops[place]
        block = rq.at[(seg + j) % 2, partner(x) % group]
        send(block, block, (t_send, t_recv), place, place, seg, partner(1))

    z_ks = range(group, n_ch, group)
    for place in cross + near[1:]:
        send(st_out.at[place], st_in.at[seg, me], (s_send, s_recv), place, me, seg, place)
    for k in z_ks:
        block = rq.at[seg, low, high]
        send(block, block, (z_send, z_recv), k // group, k // group, seg, partner(k))
    hop_refs(high, 0)
    in_q = (q_send.at[0], q_recv.at[0])
    out_q = (q_send.at[1], q_recv.at[1])
    for place, direct in zip(cross, near[n_ch // 4 :] + near[: n_ch // 4]):
        send(q_out.at[place], q_in.at[seg, me], in_q, place, me, seg, place)
        send(q_out.at[direct], q_in.at[seg, me], out_q, direct, me, other, direct)
    for place in near[1:]:
        send(q_out.at[place], q_in.at[seg, me], in_q, place, me, seg, place)

    def lines(which):
        st = st_in[which]
        centre = (
            lax.broadcasted_iota(jnp.int32, (n_ch, 1, LANES), 0) * s_dev
        ).astype(jnp.float32) + (mid_dev - mid_time)
        level = jnp.sum(st[:, 0:1, :], axis=0) / n_ch
        moment = s_dev * centre * st[:, 0:1, :] + spread_dev * st[:, 1:2, :]
        slope = jnp.sum(moment, axis=0) / spread
        return st, centre, level, slope

    def convert(which, level, slope, source, codes):
        wide = wide_here if which is seg else wide_there
        coef = st_in[which, source]
        centre = (source * s_dev).astype(jnp.float32) + (mid_dev - mid_time)
        first = coef[0:1] - level - slope * centre
        second = coef[1:2] - slope
        rest = codes.astype(jnp.int32).astype(jnp.float32) * coef[2:3]
        block = (rest + first + second * v_dev).astype(wide.dtype)
        for a in range(steps):
            row = L + source * s_dev - seg * lag_dev - a * SHIFTS
            rows = pl.ds(pl.multiple_of(row, SHIFTS), s_dev)
            wide[rows, a * c_dev : (a + 1) * c_dev] = block

    def arrive(sems, buf, k):
        remote(buf, buf, sems, k, k, seg, partner(1)).wait_recv()

    is_left = lax.broadcasted_iota(jnp.int32, (half, LANES), 1) < s_dev
    lane = lax.broadcasted_iota(jnp.int32, (1, LANES), 1)
    time_id = lax.broadcasted_iota(jnp.int32, (n_ch, n_total), 1)
    in_part = time_id // s_dev == lax.broadcasted_iota(jnp.int32, (n_ch, n_total), 0)
    ones = in_part.astype(jnp.float32)
    ramps = jnp.where(in_part, (time_id % s_dev).astype(jnp.float32) - mid_dev, 0.0)
    patterns = jnp.concatenate([ones, ramps], axis=0)

    def expand(s, plane):
        st = [st_in[s, i] for i in range(n_ch)]
        centres = [i * s_dev + mid_dev - mid_time for i in range(n_ch)]
        both = sum(st[i][3:4] for i in range(n_ch))
        moved = sum(centres[i] * st[i][3:4] for i in range(n_ch))
        ref_stat = jnp.where(
            lane < width,
            both / n_ch,
            (s_dev * pltpu.roll(moved, width, 1) + spread_dev * both) / spread,
        )
        ref_slope = pltpu.roll(ref_stat, width, 1)
        first = jnp.concatenate(
            [
                st[i][3:4] - jnp.where(lane < width, ref_stat + centres[i] * ref_slope, ref_stat)
                for i in range(n_ch)
            ],
            axis=0,
        )
        scale = jnp.concatenate([st[i][4:5] for i in range(n_ch)], axis=0)
        coefs = jnp.concatenate([first, pltpu.roll(first, width, 1)], axis=0)

        def along(rows, pattern):
            return lax.dot_general(
                rows,
                pattern,
                (((0,), (0,)), ((), ())),
                precision=lax.Precision.HIGHEST,
                preferred_element_type=jnp.float32,
            )[:width]

        maps[plane, 0] = along(scale, ones)
        maps[plane, 1] = along(coefs, patterns)

    def ref_series(s, plane):
        tops, lows = [], []
        for i in range(0, n_ch, 2):
            one = rq[s, i % group, i // group].astype(jnp.int32).astype(jnp.float32)
            two = rq[s, (i + 1) % group, (i + 1) // group].astype(jnp.int32).astype(jnp.float32)
            tops.append(jnp.where(is_left, one, pltpu.roll(two, s_dev, 1)))
            lows.append(jnp.where(is_left, pltpu.roll(one, s_dev, 1), two))
        series = jnp.concatenate(
            [jnp.concatenate(tops, axis=1), jnp.concatenate(lows, axis=1)], axis=0
        )
        return (series * maps[plane, 0] + maps[plane, 1]).astype(rt_here.dtype)

    def shift_refs(series, rt, b):
        moved = series
        if b:
            blank = jnp.zeros((width, b), rt.dtype)
            moved = jnp.concatenate([blank, series[:, : n_total - b]], axis=1)
        rt[b * width : (b + 1) * width, :] = moved

    def hop_far_refs():
        for k in z_ks:
            h = partner(k) // group
            arrive((z_send, z_recv), rq.at[seg, low, h], k // group)
            hop_refs(h, k // group)
        to_twin(0)

    def take_lines():
        for place in cross + near[1:]:
            arrive((s_send, s_recv), st_in.at[seg, place], place)
        send(st_in.at[seg], st_in.at[seg], (y_send, y_recv), 0, 0, other, me)
        return lines(seg)[2:]

    def hand_over(places):
        for place in places:
            block = q_in.at[seg, place]
            arrive(in_q, block, place)
            send(block, block, out_q, place, place, other, me)

    def pass_to_twin():
        for hop in range(1, len(hops)):
            j, x = hops[hop]
            for h in range(n_high):
                row = partner(h * group) // group
                block = rq.at[(seg + j) % 2, partner(x) % group, row]
                arrive((x_send, x_recv), block, (hop - 1) * n_high + h)
            to_twin(hop)

    def convert_here(places):
        for place in places:
            convert(seg, level, slope, place, q_in[seg, place])

    hop_far_refs()
    level, slope = take_lines()
    expand(seg, 0)
    convert(seg, level, slope, me, q_out[me])
    hand_over(cross[0:1])
    convert_here(cross[0:1])
    hand_over(cross[1:2])
    convert_here(cross[1:2])
    hand_over(cross[2:3])
    convert_here(cross[2:3])
    hand_over(cross[3:4])
    convert_here(cross[3:4])
    hand_over(cross[4:5])
    convert_here(cross[4:5])
    hand_over(cross[5:6])
    convert_here(cross[5:6])
    pass_to_twin()
    hand_over(cross[6:7])
    convert_here(cross[6:7])
    hand_over(cross[7:8])
    convert_here(cross[7:8])
    for place in near[1:]:
        arrive(in_q, q_in.at[seg, place], place)
        convert(seg, level, slope, place, q_in[seg, place])
    arrive((y_send, y_recv), st_in.at[other], 0)
    _, _, other_level, other_slope = lines(other)
    expand(other, 1)
    for place in near:
        block = q_in.at[other, place]
        arrive(out_q, block, place)
        convert(other, other_level, other_slope, place, q_in[other, place])
    for place, (j, x) in enumerate(hops):
        arrive((t_send, t_recv), rq.at[(seg + j) % 2, partner(x + 1) % group], place)

    quad = 4
    rows = quad * width

    def product(rt, wide, j):
        return jnp.dot(
            rt[j * rows : (j + 1) * rows, :],
            wide[L : L + n_total, :],
            preferred_element_type=jnp.float32,
        )

    series = ref_series(seg, 0)
    for b in range(SHIFTS):
        shift_refs(series, rt_here, b)
    series = ref_series(other, 1)
    for j in range(SHIFTS // quad):
        acc[j] = product(rt_here, wide_here, j)
        for b in range(j * quad, (j + 1) * quad):
            shift_refs(series, rt_there, b)
    for place in cross:
        block = q_in.at[other, place]
        arrive(out_q, block, place)
        convert(other, other_level, other_slope, place, q_in[other, place])
    base = (seg * lag_dev).astype(jnp.float32)
    for j in range(SHIFTS // quad):
        total = acc[j] + product(rt_there, wide_there, j)
        for a in range(steps):
            for b in range(quad):
                k = a * SHIFTS + j * quad + b
                block = total[b * width : (b + 1) * width, a * c_dev : (a + 1) * c_dev]
                out_ref[k] = block * (1.0 / (2 * (n_total - (base + k))))
    for copy in sent:
        copy.wait_send()


def wide_blocks(strain, ref_local, owners):
    my_rows = strain[0]
    s_dev, chans = my_rows.shape
    n_ch = lax.axis_size("ch")
    n_seg = lax.axis_size("seg")
    n_total = s_dev * n_ch
    c_dev = chans // n_ch
    group = max(g for g in range(1, math.isqrt(n_ch) + 1) if n_ch % g == 0)
    n_high = n_ch // group
    width = ref_local.shape[0] * ref_local.shape[1]
    lag_dev = L // n_seg
    steps = lag_dev // SHIFTS
    line = jnp.pad(owners, (0, ref_local.shape[1] - owners.shape[0]))
    picks = jnp.concatenate([ref_local, line[None]], axis=0)
    vmem = pl.BlockSpec(memory_space=pltpu.VMEM)
    dma = pltpu.SemaphoreType.DMA
    turned = pl.pallas_call(
        functools.partial(fused_kernel, n_ch, group, width),
        out_shape=jax.ShapeDtypeStruct((lag_dev, width, c_dev), jnp.float32),
        in_specs=[vmem, vmem],
        out_specs=vmem,
        scratch_shapes=[
            pltpu.SMEM(picks.shape, jnp.int32),
            pltpu.VMEM((n_ch, s_dev, c_dev), jnp.float32),
            pltpu.VMEM((n_ch, s_dev, c_dev), jnp.int16),
            pltpu.VMEM((n_ch, 5, c_dev), jnp.float32),
            pltpu.VMEM((n_seg, n_ch, s_dev, c_dev), jnp.int16),
            pltpu.VMEM((n_seg, n_ch, 5, c_dev), jnp.float32),
            pltpu.VMEM((n_seg, group, n_high, width // 2, LANES), jnp.int16),
            pltpu.VMEM((L + n_total, steps * c_dev), jnp.bfloat16),
            pltpu.VMEM((L + n_total, steps * c_dev), jnp.bfloat16),
            pltpu.VMEM((SHIFTS * width, n_total), jnp.bfloat16),
            pltpu.VMEM((SHIFTS * width, n_total), jnp.bfloat16),
            pltpu.VMEM((n_seg, 2, width, n_total), jnp.float32),
            pltpu.VMEM((SHIFTS // 4, 4 * width, steps * c_dev), jnp.float32),
            dma((1,)),
            dma((n_ch,)), dma((n_ch,)),
            dma((n_seg, n_ch)), dma((n_seg, n_ch)),
            dma((n_high,)), dma((n_high,)),
            dma((n_seg * group * n_high,)), dma((n_seg * group * n_high,)),
            dma((n_seg * group,)), dma((n_seg * group,)),
            dma((1,)), dma((1,)),
        ],
        compiler_params=pltpu.CompilerParams(
            collective_id=0, has_side_effects=True, vmem_limit_bytes=GRANT
        ),
    )(my_rows, picks)
    return turned.transpose(0, 2, 1)


def solution(mesh):
    n_seg, n_ch = mesh.shape["seg"], mesh.shape["ch"]

    def per_device(strain, ref_local, owners):
        s_dev, chans = strain.shape[1:]
        fits = (
            chans == n_ch * LANES
            and n_seg == 2
            and (L // n_seg) % SHIFTS == 0
            and 2 * s_dev == LANES
            and n_ch >= 4
            and n_ch & (n_ch - 1) == 0
            and 2 * ref_local.size == LANES
            and ref_local.shape[0] <= ref_local.shape[1]
        )
        return (wide_blocks if fits else narrow_blocks)(strain, ref_local, owners)

    in_specs = (P("seg", "ch", None), P(), P())
    out_specs = P("seg", "ch", None)
    return jax.shard_map(
        per_device, mesh=mesh, in_specs=in_specs, out_specs=out_specs, check_vma=False
    )
```

```python
import functools
import math

import jax
import jax.numpy as jnp
from jax import lax
from jax.experimental import pallas as pl
from jax.experimental.pallas import tpu as pltpu
from jax.sharding import PartitionSpec as P

L = 64
LANES = 128
SHIFTS = 16
GRANT = 24 * 1024 * 1024
STEPS = 32000.0
TINY = 1e-33
MESH = pl.DeviceIdType.MESH


def spread_2(block, axis, holder):
    block = jnp.where(lax.axis_index(axis) == holder, block, jnp.zeros_like(block))
    return lax.psum(block, axis)


def detrend_cols(series):
    n_total = series.shape[0]
    mid_time = (n_total - 1) / 2.0
    spread = n_total * (n_total * n_total - 1) / 12.0
    centred = (jnp.arange(n_total, dtype=jnp.float32) - mid_time)[:, None]
    level_val = jnp.sum(series, axis=0) / n_total
    slope_val = jnp.sum(centred * series, axis=0) / spread
    return (series - level_val - slope_val * centred).astype(jnp.bfloat16)


def owner_panels(detrended, ref_local, owners):
    pieces = []
    for panel_id in range(ref_local.shape[0]):
        own_cols = jnp.take(detrended, ref_local[panel_id], axis=1)
        pieces.append(spread_2(own_cols, "ch", owners[panel_id]))
    return jnp.concatenate(pieces, axis=1)


def narrow_blocks(strain, ref_local, owners):
    my_rows = strain[0]
    s_dev, chans = my_rows.shape
    n_ch = lax.axis_size("ch")
    n_seg = lax.axis_size("seg")
    n_total = s_dev * n_ch
    c_dev = chans // n_ch
    series = lax.all_to_all(my_rows, "ch", split_axis=1, concat_axis=0, tiled=True)
    detrended = detrend_cols(series)
    panels = owner_panels(detrended, ref_local, owners)
    width_ref = panels.shape[1]
    padded = jnp.concatenate([detrended, jnp.zeros((L, c_dev), jnp.bfloat16)], axis=0)
    blk_rows = min(512, n_total)
    n_blocks = n_total // blk_rows
    lag_dev = L // n_seg
    lag_count = lax.axis_size("seg") * lag_dev

    def add_block(blk_idx, running):
        blk_start = blk_idx * blk_rows
        window = lax.dynamic_slice_in_dim(padded, blk_start, blk_rows + lag_count - 1, 0)
        lagged = jnp.concatenate(
            [window[lag_off : lag_off + blk_rows] for lag_off in range(lag_count)], axis=1
        )
        ref_block = lax.dynamic_slice_in_dim(panels, blk_start, blk_rows, 0)
        return running + lax.dot_general(
            lagged, ref_block, (((0,), (0,)), ((), ())), preferred_element_type=jnp.float32
        )

    start_acc = jnp.zeros((lag_count * c_dev, width_ref), jnp.float32)
    running = lax.fori_loop(0, n_blocks, add_block, start_acc)
    summed = lax.psum_scatter(
        running.reshape(lag_count, c_dev, width_ref), "seg", scatter_dimension=0, tiled=True
    )
    lag_ids = (lax.axis_index("seg") * lag_dev + jnp.arange(lag_dev, dtype=jnp.int32)).astype(
        jnp.float32
    )
    return summed / (n_seg * (n_total - lag_ids))[:, None, None]


def fused_kernel(
    n_ch, group, width, strain_ref, picks_ref, out_ref,
    owners_ref, mine, q_out, st_out, q_in, st_in, rq, wide_here, wide_there, rt_here, rt_there, maps, acc,
    small_sem, s_send, s_recv, q_send, q_recv, z_send, z_recv,
    x_send, x_recv, t_send, t_recv, y_send, y_recv,
):
    seg = lax.axis_index("seg")
    me = lax.axis_index("ch")
    other = 1 - seg
    high, low = me // group, me % group
    n_high = n_ch // group
    s_dev = strain_ref.shape[0]
    c_dev = strain_ref.shape[1] // n_ch
    n_total = s_dev * n_ch
    n_panels = picks_ref.shape[0] - 1
    panel_w = width // n_panels
    lag_dev = out_ref.shape[0]
    steps = lag_dev // SHIFTS
    mid_time = (n_total - 1) / 2.0
    spread = n_total * (n_total * n_total - 1) / 12.0
    mid_dev = (s_dev - 1) / 2.0
    spread_dev = s_dev * (s_dev * s_dev - 1) / 12.0
    half = width // 2
    upper = me // (n_ch // 2)

    def flip(place, k):
        bit = 1
        while bit <= k:
            if k & bit:
                place = place + (1 - 2 * ((me // bit) % 2)) * bit
            bit *= 2
        return place

    def partner(k):
        return flip(me, k)

    def far(p):
        row = (1 - upper) * (n_high // 2) + p // group
        place = p % group
        return row * group + place // 2 * 2 + (me + place) % 2

    near = [partner(k) for k in range(n_ch // 2)]
    cross = [far(p) for p in range(n_ch // 2)]

    def remote(src, dst, sems, k_send, k_recv, seg_to, ch_to):
        return pltpu.make_async_remote_copy(
            src_ref=src,
            dst_ref=dst,
            send_sem=sems[0].at[k_send],
            recv_sem=sems[1].at[k_recv],
            device_id=(seg_to, ch_to),
            device_id_type=MESH,
        )

    sent = []

    def send(*args):
        copy = remote(*args)
        copy.start()
        sent.append(copy)

    load_owners = pltpu.make_async_copy(picks_ref, owners_ref, small_sem.at[0])
    load_owners.start()
    barrier = pltpu.get_barrier_semaphore()
    for place in near[1:]:
        pl.semaphore_signal(barrier, inc=1, device_id=(seg, place), device_id_type=MESH)
    for place in near:
        pl.semaphore_signal(barrier, inc=1, device_id=(other, place), device_id_type=MESH)
    for place in cross:
        pl.semaphore_signal(barrier, inc=1, device_id=(seg, place), device_id_type=MESH)

    for wide in (wide_here, wide_there):
        wide[n_total:, :] = jnp.zeros((L, steps * c_dev), wide.dtype)
    v_dev = lax.broadcasted_iota(jnp.int32, (s_dev, c_dev), 0).astype(jnp.float32) - mid_dev

    def code(block):
        v = v_dev[:, : block.shape[1]]
        level = jnp.sum(block, axis=0, keepdims=True) / s_dev
        slope = jnp.sum(v * block, axis=0, keepdims=True) / spread_dev
        rest = block - level - slope * v
        top = jnp.maximum(jnp.max(jnp.abs(rest), axis=0, keepdims=True), TINY)
        return level, slope, top / STEPS, jnp.round(rest * (STEPS / top))

    for o in range(n_ch):
        block = strain_ref[:, o * c_dev : (o + 1) * c_dev]
        mine[o] = block
        level, slope, scale, codes = code(block)
        q_out[o] = codes.astype(jnp.int32).astype(jnp.int16)
        st_out[o, 0:3, :] = jnp.concatenate([level, slope, scale], axis=0)

    load_owners.wait()
    blocks = jnp.concatenate(
        [mine[owners_ref[n_panels, p]] for p in range(n_panels)],
        axis=1,
    )
    targets = jnp.concatenate(
        [picks_ref[p : p + 1, :panel_w] + p * c_dev for p in range(n_panels)], axis=1
    )
    hot = (
        lax.broadcasted_iota(jnp.int32, (n_panels * c_dev, width), 0) == targets
    ).astype(jnp.float32)
    picked = jnp.dot(
        blocks, hot, precision=lax.Precision.HIGHEST, preferred_element_type=jnp.float32
    )
    level, slope, scale, codes = code(picked)
    ref_rows = jnp.concatenate(
        [jnp.concatenate([level, slope], axis=1), jnp.concatenate([scale, scale], axis=1)], axis=0
    )
    st_out[:, 3:5, :] = jnp.broadcast_to(ref_rows[None], (n_ch, 2, LANES))
    turned = codes.T
    rq[seg, low, high] = (
        jnp.concatenate([turned[:half], turned[half:]], axis=1)
        .astype(jnp.int32)
        .astype(jnp.int16)
    )
    st_in[seg, me] = st_out[me]

    pl.semaphore_wait(barrier, n_ch - 1 + len(near))

    hops = [(j, x) for j in range(2) for x in range(0, group, 2)]

    def hop_refs(h, k):
        block = rq.at[seg, low, h]
        for place, (j, x) in enumerate(hops[1:]):
            sem = place * n_high + k
            send(block, block, (x_send, x_recv), sem, sem, (seg + j) % 2, partner(x))

    def to_twin(place):
        j, x = hops[place]
        block = rq.at[(seg + j) % 2, partner(x) % group]
        send(block, block, (t_send, t_recv), place, place, seg, partner(1))

    z_ks = range(group, n_ch, group)
    for k in z_ks:
        block = rq.at[seg, low, high]
        send(block, block, (z_send, z_recv), k // group, k // group, seg, partner(k))
    hop_refs(high, 0)
    for place in cross + near[1:]:
        send(st_out.at[place], st_in.at[seg, me], (s_send, s_recv), place, me, seg, place)
    in_q = (q_send.at[0], q_recv.at[0])
    out_q = (q_send.at[1], q_recv.at[1])
    for place, direct in zip(cross, near[n_ch // 4 :] + near[: n_ch // 4]):
        send(q_out.at[place], q_in.at[seg, me], in_q, place, me, seg, place)
        send(q_out.at[direct], q_in.at[seg, me], out_q, direct, me, other, direct)
    for place in near[1:]:
        send(q_out.at[place], q_in.at[seg, me], in_q, place, me, seg, place)

    def lines(which):
        st = st_in[which]
        centre = (
            lax.broadcasted_iota(jnp.int32, (n_ch, 1, LANES), 0) * s_dev
        ).astype(jnp.float32) + (mid_dev - mid_time)
        level = jnp.sum(st[:, 0:1, :], axis=0) / n_ch
        moment = s_dev * centre * st[:, 0:1, :] + spread_dev * st[:, 1:2, :]
        slope = jnp.sum(moment, axis=0) / spread
        return st, centre, level, slope

    def convert(which, level, slope, source, codes):
        wide = wide_here if which is seg else wide_there
        coef = st_in[which, source]
        centre = (source * s_dev).astype(jnp.float32) + (mid_dev - mid_time)
        first = coef[0:1] - level - slope * centre
        second = coef[1:2] - slope
        rest = codes.astype(jnp.int32).astype(jnp.float32) * coef[2:3]
        block = (rest + first + second * v_dev).astype(wide.dtype)
        for a in range(steps):
            row = L + source * s_dev - seg * lag_dev - a * SHIFTS
            rows = pl.ds(pl.multiple_of(row, SHIFTS), s_dev)
            wide[rows, a * c_dev : (a + 1) * c_dev] = block

    def arrive(sems, buf, k):
        remote(buf, buf, sems, k, k, seg, partner(1)).wait_recv()

    is_left = lax.broadcasted_iota(jnp.int32, (half, LANES), 1) < s_dev
    lane = lax.broadcasted_iota(jnp.int32, (1, LANES), 1)
    time_id = lax.broadcasted_iota(jnp.int32, (n_ch, n_total), 1)
    in_part = time_id // s_dev == lax.broadcasted_iota(jnp.int32, (n_ch, n_total), 0)
    ones = in_part.astype(jnp.float32)
    ramps = jnp.where(in_part, (time_id % s_dev).astype(jnp.float32) - mid_dev, 0.0)
    patterns = jnp.concatenate([ones, ramps], axis=0)

    def expand(s, plane):
        st = [st_in[s, i] for i in range(n_ch)]
        centres = [i * s_dev + mid_dev - mid_time for i in range(n_ch)]
        both = sum(st[i][3:4] for i in range(n_ch))
        moved = sum(centres[i] * st[i][3:4] for i in range(n_ch))
        ref_stat = jnp.where(
            lane < width,
            both / n_ch,
            (s_dev * pltpu.roll(moved, width, 1) + spread_dev * both) / spread,
        )
        ref_slope = pltpu.roll(ref_stat, width, 1)
        first = jnp.concatenate(
            [
                st[i][3:4] - jnp.where(lane < width, ref_stat + centres[i] * ref_slope, ref_stat)
                for i in range(n_ch)
            ],
            axis=0,
        )
        scale = jnp.concatenate([st[i][4:5] for i in range(n_ch)], axis=0)
        coefs = jnp.concatenate([first, pltpu.roll(first, width, 1)], axis=0)

        def along(rows, pattern):
            return lax.dot_general(
                rows,
                pattern,
                (((0,), (0,)), ((), ())),
                precision=lax.Precision.HIGHEST,
                preferred_element_type=jnp.float32,
            )[:width]

        maps[plane, 0] = along(scale, ones)
        maps[plane, 1] = along(coefs, patterns)

    def ref_series(s, plane):
        tops, lows = [], []
        for i in range(0, n_ch, 2):
            one = rq[s, i % group, i // group].astype(jnp.int32).astype(jnp.float32)
            two = rq[s, (i + 1) % group, (i + 1) // group].astype(jnp.int32).astype(jnp.float32)
            tops.append(jnp.where(is_left, one, pltpu.roll(two, s_dev, 1)))
            lows.append(jnp.where(is_left, pltpu.roll(one, s_dev, 1), two))
        series = jnp.concatenate(
            [jnp.concatenate(tops, axis=1), jnp.concatenate(lows, axis=1)], axis=0
        )
        return (series * maps[plane, 0] + maps[plane, 1]).astype(rt_here.dtype)

    def shift_refs(series, rt, b):
        moved = series
        if b:
            blank = jnp.zeros((width, b), rt.dtype)
            moved = jnp.concatenate([blank, series[:, : n_total - b]], axis=1)
        rt[b * width : (b + 1) * width, :] = moved

    def hop_far_refs():
        for k in z_ks:
            h = partner(k) // group
            arrive((z_send, z_recv), rq.at[seg, low, h], k // group)
            hop_refs(h, k // group)
        to_twin(0)

    def take_lines():
        for place in cross + near[1:]:
            arrive((s_send, s_recv), st_in.at[seg, place], place)
        send(st_in.at[seg], st_in.at[seg], (y_send, y_recv), 0, 0, other, me)
        return lines(seg)[2:]

    def hand_over(places):
        for place in places:
            block = q_in.at[seg, place]
            arrive(in_q, block, place)
            send(block, block, out_q, place, place, other, me)

    def pass_to_twin():
        for hop in range(1, len(hops)):
            j, x = hops[hop]
            for h in range(n_high):
                row = partner(h * group) // group
                block = rq.at[(seg + j) % 2, partner(x) % group, row]
                arrive((x_send, x_recv), block, (hop - 1) * n_high + h)
            to_twin(hop)

    def convert_here(places):
        for place in places:
            convert(seg, level, slope, place, q_in[seg, place])

    hop_far_refs()
    level, slope = take_lines()
    expand(seg, 0)
    convert(seg, level, slope, me, q_out[me])
    hand_over(cross[0:1])
    convert_here(cross[0:1])
    hand_over(cross[1:2])
    convert_here(cross[1:2])
    hand_over(cross[2:3])
    convert_here(cross[2:3])
    hand_over(cross[3:4])
    convert_here(cross[3:4])
    hand_over(cross[4:5])
    convert_here(cross[4:5])
    hand_over(cross[5:6])
    convert_here(cross[5:6])
    pass_to_twin()
    hand_over(cross[6:7])
    convert_here(cross[6:7])
    hand_over(cross[7:8])
    convert_here(cross[7:8])
    for place in near[1:]:
        arrive(in_q, q_in.at[seg, place], place)
        convert(seg, level, slope, place, q_in[seg, place])
    arrive((y_send, y_recv), st_in.at[other], 0)
    _, _, other_level, other_slope = lines(other)
    expand(other, 1)
    for place in near:
        block = q_in.at[other, place]
        arrive(out_q, block, place)
        convert(other, other_level, other_slope, place, q_in[other, place])
    for place, (j, x) in enumerate(hops):
        arrive((t_send, t_recv), rq.at[(seg + j) % 2, partner(x + 1) % group], place)

    quad = 4
    rows = quad * width

    def product(rt, wide, j):
        return jnp.dot(
            rt[j * rows : (j + 1) * rows, :],
            wide[L : L + n_total, :],
            preferred_element_type=jnp.float32,
        )

    series = ref_series(seg, 0)
    for b in range(SHIFTS):
        shift_refs(series, rt_here, b)
    series = ref_series(other, 1)
    for j in range(SHIFTS // quad):
        acc[j] = product(rt_here, wide_here, j)
        for b in range(j * quad, (j + 1) * quad):
            shift_refs(series, rt_there, b)
    for place in cross:
        block = q_in.at[other, place]
        arrive(out_q, block, place)
        convert(other, other_level, other_slope, place, q_in[other, place])
    base = (seg * lag_dev).astype(jnp.float32)
    for j in range(SHIFTS // quad):
        total = acc[j] + product(rt_there, wide_there, j)
        for a in range(steps):
            for b in range(quad):
                k = a * SHIFTS + j * quad + b
                block = total[b * width : (b + 1) * width, a * c_dev : (a + 1) * c_dev]
                out_ref[k] = block * (1.0 / (2 * (n_total - (base + k))))
    for copy in sent:
        copy.wait_send()


def wide_blocks(strain, ref_local, owners):
    my_rows = strain[0]
    s_dev, chans = my_rows.shape
    n_ch = lax.axis_size("ch")
    n_seg = lax.axis_size("seg")
    n_total = s_dev * n_ch
    c_dev = chans // n_ch
    group = max(g for g in range(1, math.isqrt(n_ch) + 1) if n_ch % g == 0)
    n_high = n_ch // group
    width = ref_local.shape[0] * ref_local.shape[1]
    lag_dev = L // n_seg
    steps = lag_dev // SHIFTS
    line = jnp.pad(owners, (0, ref_local.shape[1] - owners.shape[0]))
    picks = jnp.concatenate([ref_local, line[None]], axis=0)
    vmem = pl.BlockSpec(memory_space=pltpu.VMEM)
    dma = pltpu.SemaphoreType.DMA
    turned = pl.pallas_call(
        functools.partial(fused_kernel, n_ch, group, width),
        out_shape=jax.ShapeDtypeStruct((lag_dev, width, c_dev), jnp.float32),
        in_specs=[vmem, vmem],
        out_specs=vmem,
        scratch_shapes=[
            pltpu.SMEM(picks.shape, jnp.int32),
            pltpu.VMEM((n_ch, s_dev, c_dev), jnp.float32),
            pltpu.VMEM((n_ch, s_dev, c_dev), jnp.int16),
            pltpu.VMEM((n_ch, 5, c_dev), jnp.float32),
            pltpu.VMEM((n_seg, n_ch, s_dev, c_dev), jnp.int16),
            pltpu.VMEM((n_seg, n_ch, 5, c_dev), jnp.float32),
            pltpu.VMEM((n_seg, group, n_high, width // 2, LANES), jnp.int16),
            pltpu.VMEM((L + n_total, steps * c_dev), jnp.bfloat16),
            pltpu.VMEM((L + n_total, steps * c_dev), jnp.bfloat16),
            pltpu.VMEM((SHIFTS * width, n_total), jnp.bfloat16),
            pltpu.VMEM((SHIFTS * width, n_total), jnp.bfloat16),
            pltpu.VMEM((n_seg, 2, width, n_total), jnp.float32),
            pltpu.VMEM((SHIFTS // 4, 4 * width, steps * c_dev), jnp.float32),
            dma((1,)),
            dma((n_ch,)), dma((n_ch,)),
            dma((n_seg, n_ch)), dma((n_seg, n_ch)),
            dma((n_high,)), dma((n_high,)),
            dma((n_seg * group * n_high,)), dma((n_seg * group * n_high,)),
            dma((n_seg * group,)), dma((n_seg * group,)),
            dma((1,)), dma((1,)),
        ],
        compiler_params=pltpu.CompilerParams(
            collective_id=0, has_side_effects=True, vmem_limit_bytes=GRANT
        ),
    )(my_rows, picks)
    return turned.transpose(0, 2, 1)


def solution(mesh):
    n_seg, n_ch = mesh.shape["seg"], mesh.shape["ch"]

    def per_device(strain, ref_local, owners):
        s_dev, chans = strain.shape[1:]
        fits = (
            chans == n_ch * LANES
            and n_seg == 2
            and (L // n_seg) % SHIFTS == 0
            and 2 * s_dev == LANES
            and n_ch >= 4
            and n_ch & (n_ch - 1) == 0
            and 2 * ref_local.size == LANES
            and ref_local.shape[0] <= ref_local.shape[1]
        )
        return (wide_blocks if fits else narrow_blocks)(strain, ref_local, owners)

    in_specs = (P("seg", "ch", None), P(), P())
    out_specs = P("seg", "ch", None)
    return jax.shard_map(
        per_device, mesh=mesh, in_specs=in_specs, out_specs=out_specs, check_vma=False
    )
```
